32 devices in a mesh: group: 2 (over y), seq: 4 (over z), dp: 2 (over x), head: 2 (over core).
Axes of the slice: x: 2, y: 2, z: 4, core: 2. Of those that a mesh axis runs over, the one named last changes fastest.
Arguments:
- query_raw: bfloat16 [4, 512, 2048], P(('group', 'dp'), 'seq', 'head'), parts along dimension 0, may hold values from -6 to 6
- key_raw: bfloat16 [4, 512, 2048], P(('group', 'dp'), 'seq', 'head'), parts along dimension 0, may hold values from -6 to 6
- value_raw: bfloat16 [4, 512, 2048], P(('group', 'dp'), 'seq', 'head'), parts along dimension 0, may hold values from -12 to 12
- conv_weight: float32 [3, 4, 2048], P(None, None, 'head'), may hold values from -2.4 to 2.4
- beta_logit: float32 [4, 16, 512], P(('group', 'dp'), 'head', 'seq'), parts along dimension 0, may hold values from -14 to 9
- cotangent: bfloat16 [4, 512, 2048], P(('group', 'dp'), 'seq', 'head'), parts along dimension 0, may hold values from -6 to 6
Outputs:
- mixed: float32 [4, 512, 2048], P(('group', 'dp'), 'seq', 'head'), parts along dimension 0
- query_grad: bfloat16 [4, 512, 2048], P(('group', 'dp'), 'seq', 'head'), parts along dimension 0
- key_grad: bfloat16 [4, 512, 2048], P(('group', 'dp'), 'seq', 'head'), parts along dimension 0
- value_grad: bfloat16 [4, 512, 2048], P(('group', 'dp'), 'seq', 'head'), parts along dimension 0
- beta_grad: float32 [4, 16, 512], P(('group', 'dp'), 'head', 'seq'), parts along dimension 0
- conv_grad: float32 [6, 4, 16, 128], P('group', None, 'head', ('seq', 'dp')), parts along dimension 0
The draws below stay inside these ranges and needn't reach their ends.
There are 2 independent parts, one for each index of `group`. The reference program is written for one: setup_inputs(seed, part) draws one part's arguments, and reference() takes and returns one part's arrays. A program takes and returns all parts, laid end to end along the dimension named above; an argument that names none is the same for every part. Nothing has to cross between parts.
All inputs are finite; a program needn't handle non-finite values.
Results may differ from the reference program's by a relative error of at most 0.0023.
Values may be sent and summed in bfloat16 or wider, within the bound.
A program may use at most 128 MiB of HBM per device.

```python
import jax
import jax.numpy as jnp
from jax import lax

DK = 128
HEADS = 16
SPAN = 64
TAPS = 4
TOKEN_COUNT = 512
BATCH = 2


def draw_beta_logit(key, part):
    tensor_dimensions = (BATCH, HEADS, TOKEN_COUNT)
    lookup_vectors = jax.random.split(jax.random.fold_in(key, 7), 5)
    slow_base = jnp.log(DK / (2.0 * TOKEN_COUNT))
    slow_share = 0.5
    random_samples = 0.8 * jax.random.normal(lookup_vectors[2], tensor_dimensions, jnp.float32)
    picker = jax.random.uniform(lookup_vectors[0], (BATCH, HEADS, 1), jnp.float32)
    slow_level = slow_base + jax.random.uniform(lookup_vectors[1], (BATCH, HEADS, 1), jnp.float32, -1.0, 1.0)
    fast_level = jax.random.uniform(lookup_vectors[3], (BATCH, HEADS, 1), jnp.float32, -1.0, 2.0)
    magnitude_factor = jnp.where(picker < slow_share, slow_level, fast_level)
    cluster_bundles = jax.random.uniform(lookup_vectors[4], tensor_dimensions, jnp.float32) < 8.0 / TOKEN_COUNT
    payload_vectors = magnitude_factor + random_samples + jnp.where(cluster_bundles, 7.0, 0.0)
    return jnp.clip(payload_vectors, -14.0, 9.0).astype(jnp.float32)


def level_of(key, extent, cuts, least, top_value):
    gain = 1.0
    for position, parts in cuts:
        heights = jax.random.uniform(jax.random.fold_in(jax.random.fold_in(key, 6), position), (parts,), jnp.float32, least / len(cuts), top_value / len(cuts))
        gain = gain * jnp.repeat(jnp.exp(heights), extent[position] // parts).reshape((-1,) + (1,) * (len(extent) - 1 - position))
    return gain


def normal_values(key, extent, scale, most, cuts=(), kind=jnp.bfloat16):
    values = scale * jax.random.normal(key, extent, jnp.float32)
    if cuts:
        values = values * level_of(key, extent, cuts, -0.22, 0.18)
    return jnp.clip(values, -most, most).astype(kind)


def setup_inputs(seed: int = 0, part: int = 0) -> dict:
    seeds = jax.random.split(jax.random.key(seed), 7)
    part_splits = jax.random.split(jax.random.fold_in(seeds[6], part), 7)
    query_raw = normal_values(part_splits[0], (BATCH, TOKEN_COUNT, HEADS * DK), 1.0, 6.0, ((0, 2), (1, 4), (2, 2)))
    key_raw = normal_values(part_splits[1], (BATCH, TOKEN_COUNT, HEADS * DK), 1.0, 6.0, ((0, 2), (1, 4), (2, 2)))
    value_raw = normal_values(part_splits[2], (BATCH, TOKEN_COUNT, HEADS * DK), 2.0, 12.0, ((0, 2), (1, 4), (2, 2)))
    conv_weight = normal_values(seeds[3], (3, TAPS, HEADS * DK), 0.6, 2.4, ((2, 2),), jnp.float32)
    beta_logit = draw_beta_logit(jax.random.fold_in(jax.random.fold_in(seeds[6], part), 71), part)
    cotangent = normal_values(part_splits[5], (BATCH, TOKEN_COUNT, HEADS * DK), 1.0, 6.0, ((0, 2), (1, 4), (2, 2)))
    return {"query_raw": query_raw, "key_raw": key_raw, "value_raw": value_raw, "conv_weight": conv_weight, "beta_logit": beta_logit, "cotangent": cotangent}


def strict_lower(count):
    return jnp.tril(jnp.ones((count, count), jnp.float32), -1)

def solve_block(lookup_vectors, payload_vectors, betas):
    count = lookup_vectors.shape[-2]
    width = lookup_vectors.shape[-1]
    inner = jnp.einsum('...id,...jd->...ij', lookup_vectors, lookup_vectors, precision=lax.Precision.HIGHEST)
    lower_part = betas[..., :, None] * inner * strict_lower(count)
    eye_block = jnp.eye(count, dtype=jnp.float32)
    inverse = eye_block - lower_part
    power_term = lower_part
    reach = 2
    while reach < count:
        power_term = jnp.einsum('...ij,...jk->...ik', power_term, power_term, precision=lax.Precision.HIGHEST)
        inverse = jnp.einsum('...ij,...jk->...ik', inverse, eye_block + power_term, precision=lax.Precision.HIGHEST)
        reach = reach * 2
    right_side = betas[..., :, None] * jnp.concatenate([lookup_vectors, payload_vectors], axis=-1)
    solved = jnp.einsum('...ij,...jk->...ik', inverse, right_side, precision=lax.Precision.HIGHEST)
    return (solved[..., :width], solved[..., width:])

def block_step(memory, inputs):
    queries, lookup_vectors, payload_vectors, betas = inputs
    w_rows, u_rows = solve_block(lookup_vectors, payload_vectors, betas)
    corrected = u_rows - jnp.einsum('...cd,...de->...ce', w_rows, memory, precision=lax.Precision.HIGHEST)
    count = lookup_vectors.shape[-2]
    causal = jnp.tril(jnp.ones((count, count), jnp.float32))
    scores = jnp.einsum('...id,...jd->...ij', queries, lookup_vectors, precision=lax.Precision.HIGHEST) * causal
    result = jnp.einsum('...cd,...de->...ce', queries, memory, precision=lax.Precision.HIGHEST)
    result = result + jnp.einsum('...ij,...je->...ie', scores, corrected, precision=lax.Precision.HIGHEST)
    memory = memory + jnp.einsum('...cd,...ce->...de', lookup_vectors, corrected, precision=lax.Precision.HIGHEST)
    return (memory, result)

def to_blocks(active, heads):
    batch, length, total = active.shape
    width = total // heads
    return active.reshape(batch, length // SPAN, SPAN, heads, width).transpose(1, 0, 3, 2, 4)

def from_blocks(blocks):
    count, batch, heads, block_len, width = blocks.shape
    return blocks.transpose(1, 0, 3, 2, 4).reshape(batch, count * block_len, heads * width)

def normalize(blocks):
    return blocks * lax.rsqrt(lax.optimization_barrier(jnp.sum(blocks * blocks, axis=-1, keepdims=True)) + 1e-06)

def prepare(query_ext, key_ext, value_ext, taps_all, logits):
    heads = logits.shape[1]
    margin = taps_all.shape[1] - 1
    length = query_ext.shape[1] - margin

    def convolve(series, taps):
        total = taps[0][None, None, :] * series[:, 0:length]
        for offset in range(1, margin + 1):
            total = total + taps[offset][None, None, :] * series[:, offset:offset + length]
        return total
    queries = normalize(to_blocks(jax.nn.silu(convolve(query_ext, taps_all[0])), heads))
    lookup_vectors = normalize(to_blocks(jax.nn.silu(convolve(key_ext, taps_all[1])), heads))
    payload_vectors = to_blocks(jax.nn.silu(convolve(value_ext, taps_all[2])), heads)
    batch = logits.shape[0]
    betas = jax.nn.sigmoid(logits).reshape(batch, heads, length // SPAN, SPAN).transpose(2, 0, 1, 3)
    return (queries, lookup_vectors, payload_vectors, betas)

def reference(query_raw, key_raw, value_raw, conv_weight, beta_logit, cotangent):
    heads = beta_logit.shape[1]
    width = query_raw.shape[2] // heads
    margin = conv_weight.shape[1] - 1

    def sequence(items):
        query_one, key_one, value_one, logit_one, cot_one = items

        def forward(query_in, key_in, value_in, taps_all, logits):
            pad_rows = jnp.zeros((margin, query_in.shape[1]), jnp.float32)
            query_ext = jnp.concatenate([pad_rows, query_in], axis=0)[None]
            key_ext = jnp.concatenate([pad_rows, key_in], axis=0)[None]
            value_ext = jnp.concatenate([pad_rows, value_in], axis=0)[None]
            blocks = prepare(query_ext, key_ext, value_ext, taps_all, logits[None])
            start = jnp.zeros((1, heads, width, width), jnp.float32)
            final, outputs = lax.scan(block_step, start, blocks)
            return from_blocks(outputs)[0]
        mixed_one, pullback = jax.vjp(forward, query_one.astype(jnp.float32), key_one.astype(jnp.float32), value_one.astype(jnp.float32), conv_weight, logit_one)
        grads = pullback(cot_one.astype(jnp.float32))
        return (mixed_one, grads[0].astype(jnp.bfloat16), grads[1].astype(jnp.bfloat16), grads[2].astype(jnp.bfloat16), grads[4], grads[3])
    results = lax.map(sequence, (query_raw, key_raw, value_raw, beta_logit, cotangent))
    conv_grad = lax.optimization_barrier(jnp.sum(results[5], axis=0)).reshape(3, conv_weight.shape[1], heads, width)
    return (results[0], results[1], results[2], results[3], results[4], conv_grad)
```

```python
import functools
import itertools

import jax
import jax.numpy as jnp
from jax import lax
from jax.experimental import pallas as pl
from jax.experimental.pallas import tpu as pltpu
from jax.sharding import PartitionSpec as P

MESH = pl.DeviceIdType.MESH
F32 = jnp.float32
BF16 = jnp.bfloat16
SKEW = 3
GROUP = 4
PAIR = 2
REST = 4
RAISE = 16384.0


def split(x):
    high = x.astype(BF16)
    return high, (x - high.astype(F32)).astype(BF16)


def whole(x):
    return x.astype(BF16), None


def mm(a, b, flip=False):
    ah, al = a
    bh, bl = b
    lhs = ah if al is None else jnp.concatenate([ah, al], axis=1)
    if flip:
        axis_n, axis_k = 0, 1
    else:
        axis_n, axis_k = 1, 0
    n = bh.shape[axis_n]
    rhs = bh if bl is None else jnp.concatenate([bh, bl], axis=axis_n)
    if al is not None:
        rhs = jnp.concatenate([rhs, rhs], axis=axis_k)
    out = lax.dot_general(
        lhs, rhs, (((1,), (axis_k,)), ((), ())), preferred_element_type=F32
    )
    if bl is not None:
        out = out[:, :n] + out[:, n:]
    return out


def encode(x):
    x = x * RAISE
    square = x * x
    return (x * jnp.abs(x) * square).astype(BF16)


def decode(code):
    code = code.astype(F32)
    size = jnp.abs(code)
    root = jnp.where(size > 0.0, lax.rsqrt(lax.rsqrt(size)), 0.0) * (1.0 / RAISE)
    return jnp.where(code < 0.0, -root, root)


def kernel(
    shards, parts, scatter,
    q_hbm, k_hbm, v_hbm, conv_hbm, beta_hbm, cot_hbm,
    mixed_ref, dq_ref, dk_ref, dv_ref, dbeta_ref, conv_out,
    q_raw, k_raw, v_raw, conv_ref, beta_ref, cot_ref,
    halo, q_s, k_s, v_s, g_s, p_s, gram_s, inv_s, wu_s, r_s, n_s, nt_s,
    loc_state, loc_adj, out_state, out_adj, in_state, in_adj, edge_out, edge_in, tail, cg, cgt, gathered,
    halo_send, halo_recv, state_send, state_recv, adj_send, adj_recv,
    edge_send, edge_recv, cg_send, cg_recv, load_sem, beside,
):
    z = lax.axis_index("seq")
    heads = beta_ref.shape[0]
    count, width = q_raw.shape[0], q_raw.shape[1] // heads
    first, last = z == 0, z == shards - 1
    raws = (q_raw, k_raw, v_raw)
    sources = (q_hbm, k_hbm, v_hbm, conv_hbm, beta_hbm, cot_hbm)
    loads = [
        pltpu.make_async_copy(source, kept, load_sem.at[i])
        for i, (source, kept) in enumerate(
            zip(sources, (q_raw, k_raw, v_raw, conv_ref, beta_ref, cot_ref))
        )
    ]
    for load in loads:
        load.start()
    grads = (dq_ref, dk_ref, dv_ref)

    barrier = pltpu.get_barrier_semaphore()
    if scatter:
        total = shards * parts
        column = lax.axis_index("dp")
        mine = z * parts + column

        def peer_of(step):
            peer = lax.rem(mine + step, total)
            return peer, {"seq": peer // parts, "dp": lax.rem(peer, parts)}

        def beside_of(step):
            return {"dp": lax.rem(column + step, parts)}

        for step in range(1, parts):
            pl.semaphore_signal(
                barrier, inc=1, device_id=beside_of(step), device_id_type=MESH
            )

    @pl.when(z > 0)
    def _():
        pl.semaphore_signal(barrier, inc=1, device_id={"seq": z - 1}, device_id_type=MESH)

    @pl.when(z < shards - 1)
    def _():
        pl.semaphore_signal(barrier, inc=1, device_id={"seq": z + 1}, device_id_type=MESH)

    met = parts - 1 if scatter else 0

    @pl.when((z > 0) & (z < shards - 1))
    def _():
        pl.semaphore_wait(barrier, met + 2)

    @pl.when(first | last)
    def _():
        pl.semaphore_wait(barrier, met + 1)

    def halo_copy(s):
        return pltpu.make_async_remote_copy(
            src_ref=sources[s].at[pl.ds(count - 16, 16), :], dst_ref=halo.at[s],
            send_sem=halo_send.at[s], recv_sem=halo_recv.at[s],
            device_id={"seq": z + 1}, device_id_type=MESH,
        )

    def state_copy(h):
        return pltpu.make_async_remote_copy(
            src_ref=out_state.at[h], dst_ref=in_state.at[h],
            send_sem=state_send.at[h], recv_sem=state_recv.at[h],
            device_id={"seq": z + 1}, device_id_type=MESH,
        )

    def adj_copy(h):
        return pltpu.make_async_remote_copy(
            src_ref=out_adj.at[h], dst_ref=in_adj.at[h],
            send_sem=adj_send.at[h], recv_sem=adj_recv.at[h],
            device_id={"seq": z - 1}, device_id_type=MESH,
        )

    def edge_copy(h):
        return pltpu.make_async_remote_copy(
            src_ref=edge_out.at[h], dst_ref=edge_in.at[h],
            send_sem=edge_send.at[h], recv_sem=edge_recv.at[h],
            device_id={"seq": z - 1}, device_id_type=MESH,
        )

    @pl.when(z < shards - 1)
    def _():
        for s in range(3):
            halo_copy(s).start()

    @pl.when(first)
    def _():
        halo[...] = jnp.zeros_like(halo)
        in_state[...] = jnp.zeros_like(in_state)

    @pl.when(last)
    def _():
        in_adj[...] = jnp.zeros_like(in_adj)
        edge_in[...] = jnp.zeros_like(edge_in)

    cg[...] = jnp.zeros_like(cg)
    rows = lax.broadcasted_iota(jnp.int32, (count, count), 0)
    cols = lax.broadcasted_iota(jnp.int32, (count, count), 1)
    apart = rows ^ cols
    strict = rows > cols
    lower = rows >= cols
    eye = rows == cols

    def beta_of(h):
        row = 1.0 / (1.0 + jnp.exp(-beta_ref[pl.ds(h, 1), :]))
        return row, jnp.sum(jnp.where(eye, row, 0.0), axis=1, keepdims=True)

    def lanes_of(h):
        return pl.ds(pl.multiple_of(h * width, width), width)

    def series_of(s, h):
        before = halo[s, :, lanes_of(h)].astype(F32)[8:]
        return jnp.concatenate([before, raws[s][:, lanes_of(h)].astype(F32)], axis=0)

    for load in loads:
        load.wait()

    @pl.when(z > 0)
    def _():
        for s in range(3):
            halo_copy(s).wait_recv()

    def prepare(step, carry):
        ids = [step * GROUP + i for i in range(GROUP)]
        qs, ks, vs = [], [], []
        for h in ids:
            lanes = lanes_of(h)
            made = []
            for s in range(3):
                ext = series_of(s, h)
                pre = conv_ref[s, 0:1, lanes] * ext[5:5 + count]
                for j in range(1, 4):
                    pre = pre + conv_ref[s, j:j + 1, lanes] * ext[5 + j:5 + j + count]
                gate = 1.0 / (1.0 + jnp.exp(-pre))
                act = pre * gate
                slope = gate * (1.0 + pre * (1.0 - gate))
                if s < 2:
                    scale = lax.rsqrt(jnp.sum(act * act, axis=1, keepdims=True) + 1e-06)
                    act = act * scale
                    slope = slope * scale
                g_s[s, h] = slope
                made.append(act)
            q_s[h], k_s[h], v_s[h] = made
            qs.append(made[0])
            ks.append(made[1])
            vs.append(made[2])
        k2 = [split(k) for k in ks]
        gram = [mm(k, k, True) for k in k2]
        score = [jnp.where(lower, mm(split(q), k, True), 0.0) for q, k in zip(qs, k2)]
        betas = [beta_of(h) for h in ids]
        low = [jnp.where(strict, b[1] * g, 0.0) for b, g in zip(betas, gram)]
        inv = [jnp.where(eye, 1.0, 0.0) - jnp.where(apart < 2, a, 0.0) for a in low]
        size = 2
        while size < count:
            band = (apart >= size) & (apart < 2 * size)
            i2 = [split(m) for m in inv]
            part = [mm(split(jnp.where(band, a, 0.0)), m) for a, m in zip(low, i2)]
            inv = [m - mm(n, split(x)) for m, n, x in zip(inv, i2, part)]
            size *= 2
        wu = [
            mm(split(m * b[0]), split(jnp.concatenate([k, v], axis=1)))
            for m, b, k, v in zip(inv, betas, ks, vs)
        ]
        nb = [mm(split(k.T), split(x)) for k, x in zip(ks, wu)]
        reader = [q - mm(split(p), split(x[:, :width])) for q, p, x in zip(qs, score, wu)]
        source = [
            mm(split(r.T), (cot_ref[:, lanes_of(h)], None)) for r, h in zip(reader, ids)
        ]
        for i, h in enumerate(ids):
            loc_state[h] = nb[i][:, width:]
            loc_adj[h] = source[i]
            p_s[h] = score[i]
            gram_s[h] = gram[i]
            inv_s[h] = inv[i]
            wu_s[h] = wu[i]
            r_s[h] = reader[i]
            n_s[h] = jnp.concatenate(split(nb[i][:, :width]), axis=1)
            nt_s[h] = jnp.concatenate(split(nb[i][:, :width].T), axis=1)

        @pl.when(first)
        def _():
            for i, h in enumerate(ids):
                out_state[h] = encode(nb[i][:, width:])
                state_copy(h).start()

        @pl.when(last)
        def _():
            for i, h in enumerate(ids):
                out_adj[h] = encode(source[i])
                adj_copy(h).start()

        return carry

    lax.fori_loop(0, heads // GROUP, prepare, 0)

    def advance(pair, value):
        high, low = split(value)
        both = jnp.concatenate([high, low], axis=1)
        out = jnp.dot(pair, jnp.concatenate([both, both], axis=0), preferred_element_type=F32)
        return value - (out[:, :width] + out[:, width:])

    def finish(h):
        lanes = lanes_of(h)
        cot = cot_ref[:, lanes]
        query, key, value = q_s[h], k_s[h], v_s[h]
        score, wu, reader = p_s[h], wu_s[h], r_s[h]
        w_rows, u_rows = wu[:, :width], wu[:, width:]
        state2, adj2 = split(decode(in_state[h])), split(decode(in_adj[h]))
        key2 = split(key)
        beta_row, beta_col = beta_of(h)
        reads = mm(split(jnp.concatenate([w_rows, reader], axis=0)), state2)
        yield
        corrected = u_rows - reads[:count]
        mixed_ref[:, lanes] = reads[count:] + mm(split(score), split(u_rows))
        d_corr = mm(split(score.T), (cot, None)) + mm(key2, adj2)
        yield
        corr2 = split(corrected)
        d_score = jnp.where(lower, mm((cot, None), corr2, True), 0.0)
        yield
        back = mm(split(jnp.concatenate([cot.astype(F32), d_corr], axis=0)), state2, True)
        yield
        y = mm(split(inv_s[h].T), split(jnp.concatenate([-back[count:], d_corr], axis=1)))
        y_k, y_v = y[:, :width], y[:, width:]
        yield
        d_low = jnp.where(strict, -mm(split(y), split(wu), True), 0.0)
        yield
        d_beta = jnp.sum(y_k * key + y_v * value + d_low * gram_s[h], axis=1, keepdims=True)
        d_gram = beta_col * d_low
        onto = mm(split(jnp.concatenate([d_score, d_gram + d_gram.T], axis=0)), key2)
        yield
        d_query = back[:count] + onto[:count]
        d_key = (
            mm(split(d_score.T), split(query)) + mm(corr2, adj2, True)
            + beta_col * y_k + onto[count:]
        )
        yield
        d_value = beta_col * y_v
        d_row = jnp.sum(jnp.where(eye, d_beta, 0.0), axis=0, keepdims=True)
        dbeta_ref[pl.ds(h, 1), :] = d_row * beta_row * (1.0 - beta_row)
        blank = jnp.zeros((8, width), F32)
        for s, grad in enumerate((d_query, d_key, d_value)):
            if s < 2:
                unit = (query, key)[s]
                grad = grad - unit * jnp.sum(grad * unit, axis=1, keepdims=True)
            d_pre = grad * g_s[s, h]
            ext = jnp.concatenate([blank, d_pre, blank], axis=0)
            yield
            series = series_of(s, h)
            full = None
            for j in range(4):
                moved = ext[3 - j:3 - j + count + 8]
                term = conv_ref[s, j:j + 1, lanes] * moved
                full = term if full is None else full + term
                cg[pl.ds((s * 4 + j) * heads + h, 1), :] = jnp.sum(
                    series * moved, axis=0, keepdims=True
                )
            edge_out[h, s * 8:s * 8 + 8, :] = full[:8]
            grads[s][:, lanes] = full[8:].astype(BF16)
            tail[h, s * 8:s * 8 + 8, :] = full[count:]

    early = z < shards // 2
    lag_state = jnp.where(early, 0, SKEW)
    lag_end = jnp.where(first | last, SKEW, SKEW + REST)
    lag_adj = jnp.where(early, SKEW, 0)

    def chain(step, carry):
        hs = step - lag_state
        ha = step - lag_adj

        @pl.when((hs >= 0) & (hs < heads) & (z > 0))
        def _():
            state_copy(hs).wait_recv()

            @pl.when(z < shards - 1)
            def _():
                out_state[hs] = encode(loc_state[hs] + advance(n_s[hs], decode(in_state[hs])))
                state_copy(hs).start()

        @pl.when((ha >= 0) & (ha < heads) & (z < shards - 1))
        def _():
            adj_copy(ha).wait_recv()

            @pl.when(z > 0)
            def _():
                out_adj[ha] = encode(loc_adj[ha] + advance(nt_s[ha], decode(in_adj[ha])))
                adj_copy(ha).start()

        done = step - lag_end

        @pl.when((done >= 0) & (done < heads) & (lax.rem(done, PAIR) == PAIR - 1))
        def _():
            ids = [done - PAIR + 1 + i for i in range(PAIR)]
            for _ in itertools.zip_longest(*[finish(h) for h in ids]):
                pass

            @pl.when(z > 0)
            def _():
                for h in ids:
                    edge_copy(h).start()

        if scatter:
            @pl.when(step == SKEW)
            def _():
                for other in range(1, parts):
                    pl.semaphore_signal(
                        beside, inc=1, device_id=beside_of(other), device_id_type=MESH
                    )

        return carry

    lax.fori_loop(0, heads + SKEW + REST, chain, 0)

    if scatter:
        if parts > 1:
            pl.semaphore_wait(beside, parts - 1)
        piece = cgt.shape[0] // total
        cgt[...] = cg[...].T

        def cg_copy(step):
            peer, where = peer_of(step)
            return pltpu.make_async_remote_copy(
                src_ref=cgt.at[pl.ds(pl.multiple_of(peer * piece, 8), piece), :],
                dst_ref=gathered.at[step],
                send_sem=cg_send.at[step], recv_sem=cg_recv.at[step],
                device_id=where, device_id_type=MESH,
            )

        for step in range(1, total):
            cg_copy(step).start()

    @pl.when(z < shards - 1)
    def _():
        def take(h, carry):
            edge_copy(h).wait_recv()
            return carry

        lax.fori_loop(0, heads, take, 0)

    for h in range(heads):
        for s in range(3):
            lanes = slice(h * width, (h + 1) * width)
            extra = tail[h, s * 8:s * 8 + 8, :] + edge_in[h, s * 8:s * 8 + 8, :]
            grads[s][count - 8:, lanes] = extra.astype(BF16)

    if scatter:
        sums = cgt[pl.ds(pl.multiple_of(mine * piece, 8), piece), :]
        for step in range(1, total):
            cg_copy(step).wait_recv()
            sums = sums + gathered[step]
        conv_out[...] = sums
        for step in range(1, total):
            cg_copy(step).wait_send()
    else:
        conv_out[...] = cg[...]

    @pl.when(z < shards - 1)
    def _():
        for s in range(3):
            halo_copy(s).wait_send()

        def sent(h, carry):
            state_copy(h).wait_send()
            return carry

        lax.fori_loop(0, heads, sent, 0)

    @pl.when(z > 0)
    def _():
        def sent(h, carry):
            adj_copy(h).wait_send()
            edge_copy(h).wait_send()
            return carry

        lax.fori_loop(0, heads, sent, 0)


def flush(count, *refs):
    blocks, rest = refs[:count], refs[count:]
    if len(rest) == count + 1:
        outs, sems = rest[:count], rest[count]
        extra = ()
    else:
        conv, outs, conv_out, sems, turned = rest[0], rest[1:count + 1], *rest[count + 1:]
        extra = ((turned, conv_out),)
    copies = [
        pltpu.make_async_copy(block, out, sems.at[i])
        for i, (block, out) in enumerate((*zip(blocks, outs), *extra))
    ]
    for copy in copies[:count]:
        copy.start()
    if extra:
        turned[...] = conv[...].T[:turned.shape[0]]
        copies[count].start()
    for copy in copies:
        copy.wait()


def per_device(query_raw, key_raw, value_raw, conv_weight, beta_logit, cotangent):
    shards, parts = lax.axis_size("seq"), lax.axis_size("dp")
    heads = beta_logit.shape[1]
    count, channels = query_raw.shape[1:]
    width = channels // heads
    taps = conv_weight.shape[1]
    total = shards * parts
    scatter = total > 1 and width % (8 * total) == 0
    piece = width // total if scatter else 8
    slots = total if scatter else 2
    square = lambda dtype=F32, cols=width: pltpu.VMEM((heads, count, cols), dtype)
    dma = pltpu.SemaphoreType.DMA
    vmem = pl.BlockSpec(memory_space=pltpu.VMEM)
    conv_rows = piece if scatter else width
    outs = pl.pallas_call(
        functools.partial(kernel, shards, parts, scatter),
        out_shape=(
            jax.ShapeDtypeStruct((count, channels), F32),
            jax.ShapeDtypeStruct((count, channels), BF16),
            jax.ShapeDtypeStruct((count, channels), BF16),
            jax.ShapeDtypeStruct((count, channels), BF16),
            jax.ShapeDtypeStruct((heads, count), F32),
            jax.ShapeDtypeStruct((conv_rows, 128), F32),
        ),
        in_specs=[pl.BlockSpec(memory_space=pltpu.HBM)] * 6,
        out_specs=[vmem] * 6,
        scratch_shapes=[
            pltpu.VMEM((count, channels), BF16),
            pltpu.VMEM((count, channels), BF16),
            pltpu.VMEM((count, channels), BF16),
            pltpu.VMEM((3, taps, channels), F32),
            pltpu.VMEM((heads, count), F32),
            pltpu.VMEM((count, channels), BF16),
            pltpu.VMEM((3, 16, channels), BF16),
            square(), square(), square(),
            pltpu.VMEM((3, heads, count, width), F32),
            square(), square(), square(), square(F32, 2 * width), square(),
            square(BF16, 2 * width), square(BF16, 2 * width),
            square(), square(),
            square(BF16), square(BF16), square(BF16), square(BF16),
            pltpu.VMEM((heads, 24, width), F32),
            pltpu.VMEM((heads, 24, width), F32),
            pltpu.VMEM((heads, 24, width), F32),
            pltpu.VMEM((128, width), F32),
            pltpu.VMEM((width, 128), F32),
            pltpu.VMEM((slots, piece, 128), F32),
            dma((3,)), dma((3,)),
            dma((heads,)), dma((heads,)), dma((heads,)), dma((heads,)),
            dma((heads,)), dma((heads,)), dma((slots,)), dma((slots,)), dma((6,)),
            pltpu.SemaphoreType.REGULAR,
        ],
        compiler_params=pltpu.CompilerParams(
            collective_id=0, has_side_effects=True, vmem_limit_bytes=48 << 20
        ),
    )(
        *(
            pltpu.with_memory_space_constraint(x, pltpu.HBM)
            for x in (
                query_raw[0], key_raw[0], value_raw[0],
                conv_weight, beta_logit[0], cotangent[0],
            )
        )
    )
    used = 3 * taps * heads
    blocks, conv = outs[:5], outs[5]
    held, free = pl.BlockSpec(memory_space=pl.ANY), pl.BlockSpec(memory_space=pltpu.HBM)
    extra_shape = (jax.ShapeDtypeStruct((used, piece), F32),) if scatter else ()
    flushed = pl.pallas_call(
        functools.partial(flush, 5),
        out_shape=(*(jax.ShapeDtypeStruct(x.shape, x.dtype) for x in blocks), *extra_shape),
        in_specs=[held] * 5 + [vmem] * len(extra_shape),
        out_specs=[free] * (5 + len(extra_shape)),
        scratch_shapes=[
            dma((5 + len(extra_shape),)),
            *(pltpu.VMEM(x.shape, F32) for x in extra_shape),
        ],
        compiler_params=pltpu.CompilerParams(vmem_limit_bytes=2 << 20),
    )(*blocks, *((conv,) if scatter else ()))
    mixed, d_query, d_key, d_value, d_beta = flushed[:5]
    if scatter:
        conv_grad = flushed[5].reshape(3, taps, heads, piece)
    else:
        conv_grad = lax.psum_scatter(
            conv[:used].reshape(3, taps, heads, width),
            ("seq", "dp"), scatter_dimension=3, tiled=True,
        )
    return (mixed[None], d_query[None], d_key[None], d_value[None], d_beta[None], conv_grad)


def solution(mesh):
    rows = P(("group", "dp"), "seq", "head")
    in_specs = (
        rows, rows, rows,
        P(None, None, "head"),
        P(("group", "dp"), "head", "seq"),
        rows,
    )
    out_specs = (
        rows, rows, rows, rows,
        P(("group", "dp"), "head", "seq"),
        P("group", None, "head", ("seq", "dp")),
    )
    return jax.shard_map(
        per_device, mesh=mesh, in_specs=in_specs, out_specs=out_specs, check_vma=False
    )
```

```python
import functools
import itertools

import jax
import jax.numpy as jnp
from jax import lax
from jax.experimental import pallas as pl
from jax.experimental.pallas import tpu as pltpu
from jax.sharding import PartitionSpec as P

MESH = pl.DeviceIdType.MESH
F32 = jnp.float32
BF16 = jnp.bfloat16
GROUP = 4
PAIR = 2
SKEW = 2
REST = 1
TILE = 8
RAISE = 16384.0


def pair(x):
    high = x.astype(BF16)
    return high, (x - high.astype(F32)).astype(BF16)


def left(p):
    return jnp.concatenate(p, axis=1)


def rows_of(p):
    both = jnp.concatenate(p, axis=1)
    return jnp.concatenate([both, both], axis=0)


def turned(*ps):
    return jnp.concatenate(
        [jnp.concatenate([x for p in ps for x in (p[i], p[i])], axis=1) for i in (0, 1)],
        axis=0,
    )


def flipped(p):
    return p[0].T, p[1].T


def stack(*xs):
    return jnp.concatenate(xs, axis=0)


def dot(a, b, flip=False):
    return lax.dot_general(
        a, b, (((1,), (1 if flip else 0,)), ((), ())), preferred_element_type=F32
    )


def fold(x):
    n = x.shape[1] // 2
    return x[:, :n] + x[:, n:]


def halves(ref, h):
    both = ref[h]
    n = both.shape[1] // 2
    return both[:, :n], both[:, n:]


def encode(x):
    x = x * RAISE
    square = x * x
    return (x * jnp.abs(x) * square).astype(BF16)


def decode(code):
    code = code.astype(F32)
    size = jnp.abs(code)
    root = jnp.where(size > 0.0, lax.rsqrt(lax.rsqrt(size)), 0.0) * (1.0 / RAISE)
    return jnp.where(code < 0.0, -root, root)


def kernel(
    shards, parts, scatter,
    q_hbm, k_hbm, v_hbm, conv_hbm, beta_hbm, cot_hbm,
    mixed_ref, dq_ref, dk_ref, dv_ref, dbeta_ref, conv_out,
    q_raw, k_raw, v_raw, conv_ref, beta_ref, cot_ref,
    halo_out, halo_in, before, q_s, k_s, v_s, g_s, bcol_s, gram_s, pu_s, pg_s,
    kp_s, qp_s, tp_s, wp_s, up_s, rp_s, np_s, ntp_s, masks, spread,
    loc_state, loc_adj, out_state, out_adj, in_state, in_adj,
    edge_out, edge_in, tail, cg, cgt, gathered,
    halo_send, halo_recv, state_send, state_recv, adj_send, adj_recv,
    edge_send, edge_recv, cg_send, cg_recv, load_sem, beside,
):
    z = lax.axis_index("seq")
    heads = beta_ref.shape[0]
    count, width = q_raw.shape[0], q_raw.shape[1] // heads
    first, last = z == 0, z == shards - 1
    raws = (q_raw, k_raw, v_raw)
    acts = (q_s, k_s, v_s)
    sources = (q_hbm, k_hbm, v_hbm, conv_hbm, beta_hbm, cot_hbm)
    loads = [
        pltpu.make_async_copy(source, kept, load_sem.at[i])
        for i, (source, kept) in enumerate(
            zip(sources, (q_raw, k_raw, v_raw, conv_ref, beta_ref, cot_ref))
        )
    ]
    for load in loads:
        load.start()
    grads = (dq_ref, dk_ref, dv_ref)

    barrier = pltpu.get_barrier_semaphore()
    if scatter:
        total = shards * parts
        column = lax.axis_index("dp")
        mine = z * parts + column

        def peer_of(step):
            peer = lax.rem(mine + step, total)
            return peer, {"seq": peer // parts, "dp": lax.rem(peer, parts)}

        def beside_of(step):
            return {"dp": lax.rem(column + step, parts)}

        for step in range(1, parts):
            pl.semaphore_signal(
                barrier, inc=1, device_id=beside_of(step), device_id_type=MESH
            )

    @pl.when(z > 0)
    def _():
        pl.semaphore_signal(barrier, inc=1, device_id={"seq": z - 1}, device_id_type=MESH)

    @pl.when(z < shards - 1)
    def _():
        pl.semaphore_signal(barrier, inc=1, device_id={"seq": z + 1}, device_id_type=MESH)

    met = parts - 1 if scatter else 0

    def halo_copy():
        return pltpu.make_async_remote_copy(
            src_ref=halo_out, dst_ref=halo_in,
            send_sem=halo_send, recv_sem=halo_recv,
            device_id={"seq": z + 1}, device_id_type=MESH,
        )

    def state_copy(h):
        return pltpu.make_async_remote_copy(
            src_ref=out_state.at[h], dst_ref=in_state.at[h],
            send_sem=state_send.at[h], recv_sem=state_recv.at[h],
            device_id={"seq": z + 1}, device_id_type=MESH,
        )

    def adj_copy(h):
        return pltpu.make_async_remote_copy(
            src_ref=out_adj.at[h], dst_ref=in_adj.at[h],
            send_sem=adj_send.at[h], recv_sem=adj_recv.at[h],
            device_id={"seq": z - 1}, device_id_type=MESH,
        )

    def edge_copy(h):
        return pltpu.make_async_remote_copy(
            src_ref=edge_out.at[h], dst_ref=edge_in.at[h],
            send_sem=edge_send.at[h], recv_sem=edge_recv.at[h],
            device_id={"seq": z - 1}, device_id_type=MESH,
        )

    rows = lax.broadcasted_iota(jnp.int32, (count, count), 0)
    cols = lax.broadcasted_iota(jnp.int32, (count, count), 1)
    apart = rows ^ cols
    strict = rows > cols
    lower = rows >= cols
    eye = rows == cols
    near = apart < TILE
    sizes = []
    while (TILE << len(sizes)) < count:
        sizes.append(TILE << len(sizes))
    for i, size in enumerate(sizes):
        band = (apart >= size) & (apart < 2 * size)
        masks[i] = jnp.where(band, 1.0, 0.0).astype(BF16)
    for j in range(TILE - 1):
        here = jnp.where(rows == cols - lax.rem(cols, TILE) + j, 1.0, 0.0).astype(BF16)
        spread[:, j * count:(j + 1) * count] = stack(here, here)
    cg[...] = jnp.zeros_like(cg)

    @pl.when(first)
    def _():
        in_state[...] = jnp.zeros_like(in_state)
        before[...] = jnp.zeros_like(before)

    @pl.when(last)
    def _():
        in_adj[...] = jnp.zeros_like(in_adj)
        edge_in[...] = jnp.zeros_like(edge_in)

    def lanes_of(h):
        return pl.ds(pl.multiple_of(h * width, width), width)

    for load in loads:
        load.wait()

    @pl.when(z < shards - 1)
    def _():
        ends = [raw[count - 16:, :].astype(F32)[12:] for raw in raws]
        halo_out[...] = stack(*ends, jnp.zeros_like(ends[0])).astype(BF16)

    @pl.when((z > 0) & (z < shards - 1))
    def _():
        pl.semaphore_wait(barrier, met + 2)

    @pl.when(first | last)
    def _():
        pl.semaphore_wait(barrier, met + 1)

    @pl.when(z < shards - 1)
    def _():
        halo_copy().start()

    def activate(s, h, ext, n, at):
        lanes = lanes_of(h)
        pre = conv_ref[s, 0:1, lanes] * ext[at:at + n]
        for j in range(1, 4):
            pre = pre + conv_ref[s, j:j + 1, lanes] * ext[at + j:at + j + n]
        gate = 1.0 / (1.0 + jnp.exp(-pre))
        act = pre * gate
        slope = gate * (1.0 + pre * (1.0 - gate))
        if s < 2:
            scale = lax.rsqrt(jnp.sum(act * act, axis=1, keepdims=True) + 1e-06)
            act = act * scale
            slope = slope * scale
        acts[s][h, :n] = act
        g_s[s, h, :n] = slope

    def convolve(h, carry):
        blank = jnp.zeros((8, width), F32)
        for s in range(3):
            ext = stack(blank, raws[s][:, lanes_of(h)].astype(F32))
            activate(s, h, ext, count, 5)
        row = 1.0 / (1.0 + jnp.exp(-beta_ref[pl.ds(h, 1), :]))
        column = jnp.sum(jnp.where(eye, row, 0.0), axis=1, keepdims=True)
        bcol_s[h] = jnp.broadcast_to(column, (count, width))
        return carry

    lax.fori_loop(0, heads, convolve, 0)

    @pl.when(z > 0)
    def _():
        halo_copy().wait_recv()
        ends = halo_in[...].astype(F32)
        for s in range(3):
            three = ends[4 * s + 1:4 * s + 4]
            before[s] = stack(jnp.zeros((5, three.shape[1]), F32), three)
            for h in range(heads):
                lanes = slice(h * width, (h + 1) * width)
                ext = stack(before[s, :, lanes], raws[s][:16, lanes].astype(F32)[:8])
                activate(s, h, ext, 8, 5)

    def prepare(step, carry):
        ids = [step * GROUP + i for i in range(GROUP)]
        each = range(GROUP)
        qs = [q_s[h] for h in ids]
        ks = [k_s[h] for h in ids]
        k2 = [pair(x) for x in ks]
        q2 = [pair(x) for x in qs]
        both = [
            fold(dot(stack(left(k), left(q)), turned(k), True)) for k, q in zip(k2, q2)
        ]
        gram = [x[:count] for x in both]
        p2 = [pair(jnp.where(lower, x[count:], 0.0)) for x in both]
        low = [jnp.where(strict, bcol_s[h] * g, 0.0) for h, g in zip(ids, gram)]
        l2 = [pair(x) for x in low]
        small = [
            jnp.sum(jnp.where(near, x, 0.0).reshape(count // TILE, TILE, count), axis=0)
            for x in low
        ]
        wide = dot(left(pair(stack(*small))), spread[...])
        lane8 = lax.rem(lax.broadcasted_iota(jnp.int32, (TILE, count), 1), TILE)
        row8 = lax.broadcasted_iota(jnp.int32, (TILE, count), 0)
        x8 = [jnp.where(lane8 == row8, 1.0, 0.0) for _ in each]
        for j in range(TILE - 1):
            x8 = [
                x - wide[i * TILE:(i + 1) * TILE, j * count:(j + 1) * count] * x[j:j + 1]
                for i, x in enumerate(x8)
            ]
        inv = [jnp.where(near, stack(*[x] * (count // TILE)), 0.0) for x in x8]
        for level in range(len(sizes)):
            mask = masks[level]
            i2 = [pair(x) for x in inv]
            part = [
                fold(dot(left(m), rows_of((a[0] * mask, a[1] * mask))))
                for m, a in zip(i2, l2)
            ]
            inv = [
                m - fold(dot(left(pair(x)), rows_of(n))) for m, x, n in zip(inv, part, i2)
            ]
        t2 = [pair(x) for x in inv]
        kb = [rows_of(pair(bcol_s[h] * k)) for h, k in zip(ids, ks)]
        vb = [rows_of(pair(bcol_s[h] * v_s[h])) for h in ids]
        w2 = [pair(fold(dot(left(t), x))) for t, x in zip(t2, kb)]
        u2 = [pair(fold(dot(left(t), x))) for t, x in zip(t2, vb)]
        onto = [stack(left(flipped(k)), left(p)) for k, p in zip(k2, p2)]
        on_w = [fold(dot(a, rows_of(w))) for a, w in zip(onto, w2)]
        on_u = [fold(dot(a, rows_of(u))) for a, u in zip(onto, u2)]
        r2 = [pair(q - x[count:]) for q, x in zip(qs, on_w)]
        n2 = [pair(x[:width]) for x in on_w]
        cots = [cot_ref[:, lanes_of(h)] for h in ids]
        back = [
            dot(stack(left(flipped(r)), left(flipped(p))), stack(c, c))
            for r, p, c in zip(r2, p2, cots)
        ]

        @pl.when(first)
        def _():
            for i, h in enumerate(ids):
                out_state[h] = encode(on_u[i][:width])
                state_copy(h).start()

        @pl.when(last)
        def _():
            for i, h in enumerate(ids):
                out_adj[h] = encode(back[i][:width])
                adj_copy(h).start()

        for i, h in enumerate(ids):
            loc_state[h] = on_u[i][:width]
            loc_adj[h] = back[i][:width]
            pu_s[h] = on_u[i][width:]
            pg_s[h] = back[i][width:]
            gram_s[h] = gram[i]
            kp_s[h] = left(k2[i])
            qp_s[h] = left(q2[i])
            tp_s[h] = left(flipped(t2[i]))
            wp_s[h] = left(w2[i])
            up_s[h] = left(u2[i])
            rp_s[h] = left(r2[i])
            np_s[h] = left(n2[i])
            ntp_s[h] = left(flipped(n2[i]))

        return carry

    lax.fori_loop(0, heads // GROUP, prepare, 0)

    def advance(both, value):
        return value - fold(dot(both, rows_of(pair(value))))

    def finish(h):
        lanes = lanes_of(h)
        cot = cot_ref[:, lanes]
        state2, adj2 = pair(decode(in_state[h])), pair(decode(in_adj[h]))
        k2, q2, w2, u2 = (halves(x, h) for x in (kp_s, qp_s, wp_s, up_s))
        reads = fold(dot(stack(wp_s[h], rp_s[h]), rows_of(state2)))
        d_corr = pg_s[h] + fold(dot(kp_s[h], rows_of(adj2)))
        yield
        corrected = (u2[0].astype(F32) - reads[:count]) + u2[1].astype(F32)
        mixed_ref[:, lanes] = reads[count:] + pu_s[h]
        corr2, dc2 = pair(corrected), pair(d_corr)
        yield
        zero = jnp.zeros_like(cot)
        back = fold(dot(stack(left((cot, zero)), left(dc2)), turned(state2), True))
        d_score = jnp.where(lower, fold(dot(cot, stack(*corr2), True)), 0.0)
        yield
        y_v = fold(dot(tp_s[h], rows_of(dc2)))
        y_k = fold(dot(tp_s[h], rows_of(pair(-back[count:]))))
        yield
        ys = jnp.concatenate([*pair(y_k), *pair(y_v)], axis=1)
        d_low = jnp.where(strict, -fold(dot(ys, turned(w2, u2), True)), 0.0)
        yield
        query, key, value = q_s[h], k_s[h], v_s[h]
        beta_col = bcol_s[h]
        d_beta = jnp.sum(y_k * key + y_v * value + d_low * gram_s[h], axis=1, keepdims=True)
        d_gram = beta_col * d_low
        ds2 = pair(d_score)
        onto = fold(dot(stack(left(ds2), left(pair(d_gram + d_gram.T))), rows_of(k2)))
        yield
        d_query = back[:count] + onto[:count]
        d_key = (
            fold(dot(left(flipped(ds2)), rows_of(q2))) + fold(dot(left(corr2), turned(adj2), True))
            + beta_col * y_k + onto[count:]
        )
        yield
        d_value = beta_col * y_v
        beta_row = 1.0 / (1.0 + jnp.exp(-beta_ref[pl.ds(h, 1), :]))
        d_row = jnp.sum(jnp.where(eye, d_beta, 0.0), axis=0, keepdims=True)
        dbeta_ref[pl.ds(h, 1), :] = d_row * beta_row * (1.0 - beta_row)
        blank = jnp.zeros((8, width), F32)
        for s, grad in enumerate((d_query, d_key, d_value)):
            if s < 2:
                unit = (query, key)[s]
                grad = grad - unit * jnp.sum(grad * unit, axis=1, keepdims=True)
            d_pre = grad * g_s[s, h]
            ext = jnp.concatenate([blank, d_pre, blank], axis=0)
            yield
            series = stack(before[s, :, lanes], raws[s][:, lanes].astype(F32))
            full = None
            for j in range(4):
                moved = ext[3 - j:3 - j + count + 8]
                term = conv_ref[s, j:j + 1, lanes] * moved
                full = term if full is None else full + term
                cg[pl.ds((s * 4 + j) * heads + h, 1), :] = jnp.sum(
                    series * moved, axis=0, keepdims=True
                )
            edge_out[h, s * 8:s * 8 + 8, :] = full[:8]
            grads[s][:, lanes] = full[8:].astype(BF16)
            tail[h, s * 8:s * 8 + 8, :] = full[count:]

    early = z < shards // 2
    lag_state = jnp.where(early, 0, SKEW)
    lag_end = jnp.where(first | last, SKEW, SKEW + REST)
    lag_adj = jnp.where(early, SKEW, 0)
    pairs = heads // PAIR

    def chain(step, carry):
        hs = step - lag_state
        ha = step - lag_adj

        @pl.when((hs >= 0) & (hs < pairs) & (z > 0))
        def _():
            ids = [hs * PAIR + i for i in range(PAIR)]
            for h in ids:
                state_copy(h).wait_recv()

            @pl.when(z < shards - 1)
            def _():
                new = [loc_state[h] + advance(np_s[h], decode(in_state[h])) for h in ids]
                for h, x in zip(ids, new):
                    out_state[h] = encode(x)
                for h in ids:
                    state_copy(h).start()

        @pl.when((ha >= 0) & (ha < pairs) & (z < shards - 1))
        def _():
            ids = [ha * PAIR + i for i in range(PAIR)]
            for h in ids:
                adj_copy(h).wait_recv()

            @pl.when(z > 0)
            def _():
                new = [loc_adj[h] + advance(ntp_s[h], decode(in_adj[h])) for h in ids]
                for h, x in zip(ids, new):
                    out_adj[h] = encode(x)
                for h in ids:
                    adj_copy(h).start()

        done = step - lag_end

        @pl.when((done >= 0) & (done < pairs))
        def _():
            ids = [done * PAIR + i for i in range(PAIR)]
            for _ in itertools.zip_longest(*[finish(h) for h in ids]):
                pass

            @pl.when(z > 0)
            def _():
                for h in ids:
                    edge_copy(h).start()

        if scatter:
            @pl.when(step == 1)
            def _():
                for other in range(1, parts):
                    pl.semaphore_signal(
                        beside, inc=1, device_id=beside_of(other), device_id_type=MESH
                    )

        return carry

    lax.fori_loop(0, pairs + SKEW + REST, chain, 0)

    if scatter:
        if parts > 1:
            pl.semaphore_wait(beside, parts - 1)
        piece = cgt.shape[0] // total
        cgt[...] = cg[...].T

        def cg_copy(step):
            peer, where = peer_of(step)
            return pltpu.make_async_remote_copy(
                src_ref=cgt.at[pl.ds(pl.multiple_of(peer * piece, 8), piece), :],
                dst_ref=gathered.at[step],
                send_sem=cg_send.at[step], recv_sem=cg_recv.at[step],
                device_id=where, device_id_type=MESH,
            )

        for step in range(1, total):
            cg_copy(step).start()

    @pl.when(z < shards - 1)
    def _():
        def take(h, carry):
            edge_copy(h).wait_recv()
            return carry

        lax.fori_loop(0, heads, take, 0)

    for h in range(heads):
        for s in range(3):
            lanes = slice(h * width, (h + 1) * width)
            extra = tail[h, s * 8:s * 8 + 8, :] + edge_in[h, s * 8:s * 8 + 8, :]
            grads[s][count - 8:, lanes] = extra.astype(BF16)

    if scatter:
        sums = cgt[pl.ds(pl.multiple_of(mine * piece, 8), piece), :]
        for step in range(1, total):
            cg_copy(step).wait_recv()
            sums = sums + gathered[step]
        conv_out[...] = sums
        for step in range(1, total):
            cg_copy(step).wait_send()
    else:
        conv_out[...] = cg[...]

    @pl.when(z < shards - 1)
    def _():
        halo_copy().wait_send()

        def sent(h, carry):
            state_copy(h).wait_send()
            return carry

        lax.fori_loop(0, heads, sent, 0)

    @pl.when(z > 0)
    def _():
        def sent(h, carry):
            adj_copy(h).wait_send()
            edge_copy(h).wait_send()
            return carry

        lax.fori_loop(0, heads, sent, 0)


def flush(count, *refs):
    blocks, rest = refs[:count], refs[count:]
    if len(rest) == count + 1:
        outs, sems = rest[:count], rest[count]
        extra = ()
    else:
        conv, outs, conv_out, sems, turned = rest[0], rest[1:count + 1], *rest[count + 1:]
        extra = ((turned, conv_out),)
    copies = [
        pltpu.make_async_copy(block, out, sems.at[i])
        for i, (block, out) in enumerate((*zip(blocks, outs), *extra))
    ]
    for copy in copies[:count]:
        copy.start()
    if extra:
        turned[...] = conv[...].T[:turned.shape[0]]
        copies[count].start()
    for copy in copies:
        copy.wait()


def per_device(query_raw, key_raw, value_raw, conv_weight, beta_logit, cotangent):
    shards, parts = lax.axis_size("seq"), lax.axis_size("dp")
    heads = beta_logit.shape[1]
    count, channels = query_raw.shape[1:]
    width = channels // heads
    taps = conv_weight.shape[1]
    total = shards * parts
    scatter = total > 1 and width % (8 * total) == 0
    piece = width // total if scatter else 8
    slots = total if scatter else 2
    square = lambda dtype=F32, cols=width: pltpu.VMEM((heads, count, cols), dtype)
    dma = pltpu.SemaphoreType.DMA
    vmem = pl.BlockSpec(memory_space=pltpu.VMEM)
    conv_rows = piece if scatter else width
    levels = max(1, (count // TILE - 1).bit_length())
    outs = pl.pallas_call(
        functools.partial(kernel, shards, parts, scatter),
        out_shape=(
            jax.ShapeDtypeStruct((count, channels), F32),
            jax.ShapeDtypeStruct((count, channels), BF16),
            jax.ShapeDtypeStruct((count, channels), BF16),
            jax.ShapeDtypeStruct((count, channels), BF16),
            jax.ShapeDtypeStruct((heads, count), F32),
            jax.ShapeDtypeStruct((conv_rows, 128), F32),
        ),
        in_specs=[pl.BlockSpec(memory_space=pltpu.HBM)] * 6,
        out_specs=[vmem] * 6,
        scratch_shapes=[
            pltpu.VMEM((count, channels), BF16),
            pltpu.VMEM((count, channels), BF16),
            pltpu.VMEM((count, channels), BF16),
            pltpu.VMEM((3, taps, channels), F32),
            pltpu.VMEM((heads, count), F32),
            pltpu.VMEM((count, channels), BF16),
            pltpu.VMEM((16, channels), BF16),
            pltpu.VMEM((16, channels), BF16),
            pltpu.VMEM((3, 8, channels), F32),
            square(), square(), square(),
            pltpu.VMEM((3, heads, count, width), F32),
            *[square() for _ in range(4)],
            *[square(BF16, 2 * width) for _ in range(8)],
            pltpu.VMEM((levels, count, count), BF16),
            pltpu.VMEM((2 * count, (TILE - 1) * count), BF16),
            square(), square(),
            square(BF16), square(BF16), square(BF16), square(BF16),
            pltpu.VMEM((heads, 24, width), F32),
            pltpu.VMEM((heads, 24, width), F32),
            pltpu.VMEM((heads, 24, width), F32),
            pltpu.VMEM((128, width), F32),
            pltpu.VMEM((width, 128), F32),
            pltpu.VMEM((slots, piece, 128), F32),
            dma, dma,
            dma((heads,)), dma((heads,)), dma((heads,)), dma((heads,)),
            dma((heads,)), dma((heads,)), dma((slots,)), dma((slots,)), dma((6,)),
            pltpu.SemaphoreType.REGULAR,
        ],
        compiler_params=pltpu.CompilerParams(
            collective_id=0, has_side_effects=True, vmem_limit_bytes=48 << 20
        ),
    )(
        *(
            pltpu.with_memory_space_constraint(x, pltpu.HBM)
            for x in (
                query_raw[0], key_raw[0], value_raw[0],
                conv_weight, beta_logit[0], cotangent[0],
            )
        )
    )
    used = 3 * taps * heads
    blocks, conv = outs[:5], outs[5]
    held, free = pl.BlockSpec(memory_space=pl.ANY), pl.BlockSpec(memory_space=pltpu.HBM)
    extra_shape = (jax.ShapeDtypeStruct((used, piece), F32),) if scatter else ()
    flushed = pl.pallas_call(
        functools.partial(flush, 5),
        out_shape=(*(jax.ShapeDtypeStruct(x.shape, x.dtype) for x in blocks), *extra_shape),
        in_specs=[held] * 5 + [vmem] * len(extra_shape),
        out_specs=[free] * (5 + len(extra_shape)),
        scratch_shapes=[
            dma((5 + len(extra_shape),)),
            *(pltpu.VMEM(x.shape, F32) for x in extra_shape),
        ],
        compiler_params=pltpu.CompilerParams(vmem_limit_bytes=2 << 20),
    )(*blocks, *((conv,) if scatter else ()))
    mixed, d_query, d_key, d_value, d_beta = flushed[:5]
    if scatter:
        conv_grad = flushed[5].reshape(3, taps, heads, piece)
    else:
        conv_grad = lax.psum_scatter(
            conv[:used].reshape(3, taps, heads, width),
            ("seq", "dp"), scatter_dimension=3, tiled=True,
        )
    return (mixed[None], d_query[None], d_key[None], d_value[None], d_beta[None], conv_grad)


def solution(mesh):
    rows = P(("group", "dp"), "seq", "head")
    in_specs = (
        rows, rows, rows,
        P(None, None, "head"),
        P(("group", "dp"), "head", "seq"),
        rows,
    )
    out_specs = (
        rows, rows, rows, rows,
        P(("group", "dp"), "head", "seq"),
        P("group", None, "head", ("seq", "dp")),
    )
    return jax.shard_map(
        per_device, mesh=mesh, in_specs=in_specs, out_specs=out_specs, check_vma=False
    )
```

```python
import functools
import itertools

import jax
import jax.numpy as jnp
from jax import lax
from jax.experimental import pallas as pl
from jax.experimental.pallas import tpu as pltpu
from jax.sharding import PartitionSpec as P

MESH = pl.DeviceIdType.MESH
F32 = jnp.float32
BF16 = jnp.bfloat16
GROUP = 4
LATE = 2
TILE = 8
RAISE = 16384.0


def pair(x):
    high = x.astype(BF16)
    return high, (x - high.astype(F32)).astype(BF16)


def left(p):
    return jnp.concatenate(p, axis=1)


def rows_of(p):
    both = jnp.concatenate(p, axis=1)
    return jnp.concatenate([both, both], axis=0)


def turned(*ps):
    return jnp.concatenate(
        [jnp.concatenate([x for p in ps for x in (p[i], p[i])], axis=1) for i in (0, 1)],
        axis=0,
    )


def flipped(p):
    return p[0].T, p[1].T


def stack(*xs):
    return jnp.concatenate(xs, axis=0)


def dot(a, b, flip=False):
    return lax.dot_general(
        a, b, (((1,), (1 if flip else 0,)), ((), ())), preferred_element_type=F32
    )


def fold(x):
    n = x.shape[1] // 2
    return x[:, :n] + x[:, n:]


def halves(ref, h):
    both = ref[h]
    n = both.shape[1] // 2
    return both[:, :n], both[:, n:]


def encode(x):
    x = x * RAISE
    square = x * x
    return (x * jnp.abs(x) * square).astype(BF16)


def decode(code):
    code = code.astype(F32)
    size = jnp.abs(code)
    root = jnp.where(size > 0.0, lax.rsqrt(lax.rsqrt(size)), 0.0) * (1.0 / RAISE)
    return jnp.where(code < 0.0, -root, root)


def kernel(
    shards, parts, scatter,
    q_hbm, k_hbm, v_hbm, conv_hbm, beta_hbm, cot_hbm,
    mixed_ref, dq_ref, dk_ref, dv_ref, dbeta_ref, conv_out,
    q_raw, k_raw, v_raw, conv_ref, beta_ref, cot_ref,
    halo_out, halo_in, before, q_s, k_s, v_s, g_s, bcol_s, gram_s, pu_s, pg_s,
    kp_s, qp_s, tp_s, wp_s, up_s, rp_s, np_s, ntp_s, sp_s, cp_s, yp_s, dk_s, shift_s, masks, spread,
    loc_state, loc_adj, out_state, out_adj, in_state, in_adj,
    edge_out, edge_in, tail, cg, cgt, gathered,
    halo_send, halo_recv, state_send, state_recv, adj_send, adj_recv,
    edge_send, edge_recv, cg_send, cg_recv, load_sem, beside,
):
    z = lax.axis_index("seq")
    heads = beta_ref.shape[0]
    count, width = q_raw.shape[0], q_raw.shape[1] // heads
    first, last = z == 0, z == shards - 1
    raws = (q_raw, k_raw, v_raw)
    acts = (q_s, k_s, v_s)
    sources = (q_hbm, k_hbm, v_hbm, conv_hbm, beta_hbm, cot_hbm)
    loads = [
        pltpu.make_async_copy(source, kept, load_sem.at[i])
        for i, (source, kept) in enumerate(
            zip(sources, (q_raw, k_raw, v_raw, conv_ref, beta_ref, cot_ref))
        )
    ]
    for load in loads:
        load.start()
    grads = (dq_ref, dk_ref, dv_ref)

    barrier = pltpu.get_barrier_semaphore()
    if scatter:
        total = shards * parts
        column = lax.axis_index("dp")
        mine = z * parts + column

        def peer_of(step):
            peer = lax.rem(mine + step, total)
            return peer, {"seq": peer // parts, "dp": lax.rem(peer, parts)}

        def beside_of(step):
            return {"dp": lax.rem(column + step, parts)}

        for step in range(1, parts):
            pl.semaphore_signal(
                barrier, inc=1, device_id=beside_of(step), device_id_type=MESH
            )

    @pl.when(z > 0)
    def _():
        pl.semaphore_signal(barrier, inc=1, device_id={"seq": z - 1}, device_id_type=MESH)

    @pl.when(z < shards - 1)
    def _():
        pl.semaphore_signal(barrier, inc=1, device_id={"seq": z + 1}, device_id_type=MESH)

    met = parts - 1 if scatter else 0

    def halo_copy():
        return pltpu.make_async_remote_copy(
            src_ref=halo_out, dst_ref=halo_in,
            send_sem=halo_send, recv_sem=halo_recv,
            device_id={"seq": z + 1}, device_id_type=MESH,
        )

    def state_copy(h):
        return pltpu.make_async_remote_copy(
            src_ref=out_state.at[h], dst_ref=in_state.at[h],
            send_sem=state_send.at[h], recv_sem=state_recv.at[h],
            device_id={"seq": z + 1}, device_id_type=MESH,
        )

    def adj_copy(h):
        return pltpu.make_async_remote_copy(
            src_ref=out_adj.at[h], dst_ref=in_adj.at[h],
            send_sem=adj_send.at[h], recv_sem=adj_recv.at[h],
            device_id={"seq": z - 1}, device_id_type=MESH,
        )

    def edge_copy(h):
        return pltpu.make_async_remote_copy(
            src_ref=edge_out.at[h], dst_ref=edge_in.at[h],
            send_sem=edge_send.at[h], recv_sem=edge_recv.at[h],
            device_id={"seq": z - 1}, device_id_type=MESH,
        )

    rows = lax.broadcasted_iota(jnp.int32, (count, count), 0)
    cols = lax.broadcasted_iota(jnp.int32, (count, count), 1)
    apart = rows ^ cols
    strict = rows > cols
    lower = rows >= cols
    eye = rows == cols
    near = apart < TILE
    sizes = []
    while (TILE << len(sizes)) < count:
        sizes.append(TILE << len(sizes))
    for i, size in enumerate(sizes):
        band = (apart >= size) & (apart < 2 * size)
        masks[i] = jnp.where(band, 1.0, 0.0).astype(BF16)
    for j in range(TILE - 1):
        here = jnp.where(rows == cols - lax.rem(cols, TILE) + j, 1.0, 0.0).astype(BF16)
        spread[:, j * count:(j + 1) * count] = stack(here, here)
    cg[...] = jnp.zeros_like(cg)

    @pl.when(first)
    def _():
        in_state[...] = jnp.zeros_like(in_state)
        before[...] = jnp.zeros_like(before)

    @pl.when(last)
    def _():
        in_adj[...] = jnp.zeros_like(in_adj)
        edge_in[...] = jnp.zeros_like(edge_in)

    def lanes_of(h):
        return pl.ds(pl.multiple_of(h * width, width), width)

    for slot in range(shift_s.shape[0]):
        shift_s[slot, :8] = jnp.zeros((8, width), F32)
        shift_s[slot, 8 + count:] = jnp.zeros((8, width), F32)

    for load in loads:
        load.wait()

    @pl.when(z < shards - 1)
    def _():
        ends = [raw[count - 16:, :].astype(F32)[12:] for raw in raws]
        halo_out[...] = stack(*ends, jnp.zeros_like(ends[0])).astype(BF16)

    def activate(s, h, piece, n):
        lanes = lanes_of(h)
        taps = [conv_ref[s, j:j + 1, lanes] for j in range(4)]
        for at in range(0, n, 8):
            pre = taps[0] * piece(at + 5)
            for j in range(1, 4):
                pre = pre + taps[j] * piece(at + j + 5)
            gate = 1.0 / (1.0 + jnp.exp(-pre))
            act = pre * gate
            slope = gate * (1.0 + pre * (1.0 - gate))
            if s < 2:
                scale = lax.rsqrt(jnp.sum(act * act, axis=1, keepdims=True) + 1e-06)
                act = act * scale
                slope = slope * scale
            acts[s][h, at:at + 8] = act
            g_s[s, h, at:at + 8] = slope

    def convolve(h, carry):
        for s in range(3):
            slot = h * 3 + s
            shift_s[slot, 8:8 + count] = raws[s][:, lanes_of(h)].astype(F32)
            activate(s, h, lambda at, slot=slot: shift_s[slot, at:at + 8], count)
        row = 1.0 / (1.0 + jnp.exp(-beta_ref[pl.ds(h, 1), :]))
        column = jnp.sum(jnp.where(eye, row, 0.0), axis=1, keepdims=True)
        bcol_s[h] = jnp.broadcast_to(column, (count, width))
        return carry

    ahead = jnp.where(first, heads * 3 // 4, 0)
    lax.fori_loop(0, ahead, convolve, 0)

    @pl.when((z > 0) & (z < shards - 1))
    def _():
        pl.semaphore_wait(barrier, met + 2)

    @pl.when(first | last)
    def _():
        pl.semaphore_wait(barrier, met + 1)

    @pl.when(z < shards - 1)
    def _():
        halo_copy().start()

    lax.fori_loop(ahead, heads, convolve, 0)

    @pl.when(z > 0)
    def _():
        halo_copy().wait_recv()
        ends = halo_in[...].astype(F32)
        for s in range(3):
            three = ends[4 * s + 1:4 * s + 4]
            before[s] = stack(jnp.zeros((5, three.shape[1]), F32), three)
            for h in range(heads):
                lanes = slice(h * width, (h + 1) * width)
                ext = stack(before[s, :, lanes], raws[s][:16, lanes].astype(F32)[:8])
                activate(s, h, lambda at, ext=ext: ext[at:at + 8], 8)

    def advance(both, value):
        return value - fold(dot(both, rows_of(pair(value))))

    quads = heads // GROUP

    def pass_state(h):
        state_copy(h).wait_recv()

        @pl.when(z < shards - 1)
        def _():
            out_state[h] = encode(loc_state[h] + advance(np_s[h], decode(in_state[h])))
            state_copy(h).start()

    def pass_adjoint(h):
        adj_copy(h).wait_recv()

        @pl.when(z > 0)
        def _():
            out_adj[h] = encode(loc_adj[h] + advance(ntp_s[h], decode(in_adj[h])))
            adj_copy(h).start()

    def forward(qs, qa, least):
        def one(i, carry):
            @pl.when((qs >= 0) & (qs < quads) & (z >= least))
            def _():
                pass_state(qs * GROUP + i)

            @pl.when((qa >= 0) & (qa < quads) & (z < shards - 1))
            def _():
                pass_adjoint(qa * GROUP + i)

            return carry

        lax.fori_loop(0, GROUP, one, 0)

    def prepare(step, carry):
        ids = [step * GROUP + i for i in range(GROUP)]
        each = range(GROUP)
        qs = [q_s[h] for h in ids]
        ks = [k_s[h] for h in ids]
        k2 = [pair(x) for x in ks]
        q2 = [pair(x) for x in qs]
        both = [
            fold(dot(stack(left(k), left(q)), turned(k), True)) for k, q in zip(k2, q2)
        ]
        gram = [x[:count] for x in both]
        p2 = [pair(jnp.where(lower, x[count:], 0.0)) for x in both]
        low = [jnp.where(strict, bcol_s[h] * g, 0.0) for h, g in zip(ids, gram)]
        l2 = [pair(x) for x in low]
        small = [
            jnp.sum(jnp.where(near, x, 0.0).reshape(count // TILE, TILE, count), axis=0)
            for x in low
        ]
        wide = dot(left(pair(stack(*small))), spread[...])
        lane8 = lax.rem(lax.broadcasted_iota(jnp.int32, (TILE, count), 1), TILE)
        row8 = lax.broadcasted_iota(jnp.int32, (TILE, count), 0)
        x8 = [jnp.where(lane8 == row8, 1.0, 0.0) for _ in each]
        for j in range(TILE - 1):
            x8 = [
                x - wide[i * TILE:(i + 1) * TILE, j * count:(j + 1) * count] * x[j:j + 1]
                for i, x in enumerate(x8)
            ]
        inv = [jnp.where(near, stack(*[x] * (count // TILE)), 0.0) for x in x8]
        for level in range(len(sizes)):
            mask = masks[level]
            i2 = [pair(x) for x in inv]
            part = [
                fold(dot(left(m), rows_of((a[0] * mask, a[1] * mask))))
                for m, a in zip(i2, l2)
            ]
            inv = [
                m - fold(dot(left(pair(x)), rows_of(n))) for m, x, n in zip(inv, part, i2)
            ]
        t2 = [pair(x) for x in inv]
        kb = [rows_of(pair(bcol_s[h] * k)) for h, k in zip(ids, ks)]
        vb = [rows_of(pair(bcol_s[h] * v_s[h])) for h in ids]
        w2 = [pair(fold(dot(left(t), x))) for t, x in zip(t2, kb)]
        u2 = [pair(fold(dot(left(t), x))) for t, x in zip(t2, vb)]
        onto = [stack(left(flipped(k)), left(p)) for k, p in zip(k2, p2)]
        on_w = [fold(dot(a, rows_of(w))) for a, w in zip(onto, w2)]
        on_u = [fold(dot(a, rows_of(u))) for a, u in zip(onto, u2)]
        r2 = [pair(q - x[count:]) for q, x in zip(qs, on_w)]
        n2 = [pair(x[:width]) for x in on_w]
        cots = [cot_ref[:, lanes_of(h)] for h in ids]
        back = [
            dot(stack(left(flipped(r)), left(flipped(p))), stack(c, c))
            for r, p, c in zip(r2, p2, cots)
        ]

        @pl.when(first)
        def _():
            for i, h in enumerate(ids):
                out_state[h] = encode(on_u[i][:width])
                state_copy(h).start()

        @pl.when(last)
        def _():
            for i, h in enumerate(ids):
                out_adj[h] = encode(back[i][:width])
                adj_copy(h).start()

        for i, h in enumerate(ids):
            loc_state[h] = on_u[i][:width]
            loc_adj[h] = back[i][:width]
            pu_s[h] = on_u[i][width:]
            pg_s[h] = back[i][width:]
            gram_s[h] = gram[i]
            kp_s[h] = left(k2[i])
            qp_s[h] = left(q2[i])
            tp_s[h] = left(flipped(t2[i]))
            wp_s[h] = left(w2[i])
            up_s[h] = left(u2[i])
            rp_s[h] = left(r2[i])
            np_s[h] = left(n2[i])
            ntp_s[h] = left(flipped(n2[i]))

        @pl.when(z == 1)
        def _():
            forward(step, -1, 1)

        return carry

    lax.fori_loop(0, heads // GROUP, prepare, 0)

    def conv_back(s, h, grad):
        lanes, slot = lanes_of(h), h * 3 + s
        if s < 2:
            unit = acts[s][h]
            grad = grad - unit * jnp.sum(grad * unit, axis=1, keepdims=True)
        shift_s[slot, 8:8 + count] = grad * g_s[s, h]
        yield
        taps = [conv_ref[s, j:j + 1, lanes] for j in range(4)]
        sums = [None] * 4
        for at in range(0, count + 8, 8):
            if at == 0:
                series = before[s, :, lanes]
            elif at % 16 == 8:
                both = raws[s][at - 8:at + 8, lanes].astype(F32)
                series = both[:8]
            else:
                series = both[8:]
            full = None
            for j in range(4):
                moved = shift_s[slot, at + 3 - j:at + 11 - j]
                term, product = taps[j] * moved, series * moved
                full = term if full is None else full + term
                sums[j] = product if sums[j] is None else sums[j] + product
            if at == 0:
                edge_out[h, s * 8:s * 8 + 8, :] = full
            elif at % 16 == 8:
                held = full
            else:
                grads[s][at - 16:at, lanes] = stack(held, full).astype(BF16)
        tail[h, s * 8:s * 8 + 8, :] = full
        for j in range(4):
            cg[pl.ds((s * 4 + j) * heads + h, 1), :] = jnp.sum(sums[j], axis=0, keepdims=True)

    def state_part(h, keep):
        lanes = lanes_of(h)
        cot = cot_ref[:, lanes]
        state2 = pair(decode(in_state[h]))
        k2, q2, u2 = (halves(x, h) for x in (kp_s, qp_s, up_s))
        reads = fold(dot(stack(wp_s[h], rp_s[h]), rows_of(state2)))
        d_query = fold(dot(cot, stack(*state2), True))
        yield
        mixed_ref[:, lanes] = reads[count:] + pu_s[h]
        corr2 = pair((u2[0].astype(F32) - reads[:count]) + u2[1].astype(F32))
        yield
        ds2 = pair(jnp.where(lower, fold(dot(cot, stack(*corr2), True)), 0.0))
        yield
        d_query = d_query + fold(dot(left(ds2), rows_of(k2)))
        d_key = fold(dot(left(flipped(ds2)), rows_of(q2)))
        keep.update(state2=state2, corr2=corr2, d_key=d_key)
        yield
        yield from conv_back(0, h, d_query)

    def adjoint_part(h, keep):
        adj2 = pair(decode(in_adj[h]))
        d_corr = pg_s[h] + fold(dot(kp_s[h], rows_of(adj2)))
        dc2 = pair(d_corr)
        yield
        y_v = fold(dot(tp_s[h], rows_of(dc2)))
        yv2 = pair(y_v)
        d_beta = y_v * v_s[h]
        keep.update(adj2=adj2, dc2=dc2, yv2=yv2, d_beta=d_beta)
        yield
        yield from conv_back(2, h, bcol_s[h] * y_v)

    def last_part(h, keep):
        k2, w2, u2 = (halves(x, h) for x in (kp_s, wp_s, up_s))
        back = fold(dot(left(keep["dc2"]), turned(keep["state2"]), True))
        yield
        y_k = fold(dot(tp_s[h], rows_of(pair(-back))))
        yield
        ys = jnp.concatenate([*pair(y_k), *keep["yv2"]], axis=1)
        d_low = jnp.where(strict, -fold(dot(ys, turned(w2, u2), True)), 0.0)
        yield
        key, beta_col = k_s[h], bcol_s[h]
        d_beta = jnp.sum(
            y_k * key + keep["d_beta"] + d_low * gram_s[h], axis=1, keepdims=True
        )
        d_gram = beta_col * d_low
        d_key = (
            keep["d_key"] + beta_col * y_k
            + fold(dot(left(keep["corr2"]), turned(keep["adj2"]), True))
            + fold(dot(left(pair(d_gram + d_gram.T)), rows_of(k2)))
        )
        yield
        beta_row = 1.0 / (1.0 + jnp.exp(-beta_ref[pl.ds(h, 1), :]))
        d_row = jnp.sum(jnp.where(eye, d_beta, 0.0), axis=0, keepdims=True)
        dbeta_ref[pl.ds(h, 1), :] = d_row * beta_row * (1.0 - beta_row)
        yield from conv_back(1, h, d_key)

    def together(gens):
        for _ in itertools.zip_longest(*gens):
            pass

    def chained(*gens):
        for gen in gens:
            yield from gen

    early = z < shards // 2
    lag = jnp.where(first | last, LATE, jnp.where(early, LATE - 1, 0))

    def group_of(q):
        return [q * GROUP + i for i in range(GROUP)]

    def send_edges(ids):
        @pl.when(z > 0)
        def _():
            for h in ids:
                edge_copy(h).start()

    def chain(step, carry):
        done = step - LATE

        @pl.when(early)
        def _():
            forward(step, step - lag, 2)

            @pl.when(step < quads)
            def _():
                ids = group_of(step)
                keeps = [{} for _ in ids]
                together([state_part(h, keep) for h, keep in zip(ids, keeps)])
                for h, keep in zip(ids, keeps):
                    sp_s[h] = left(keep["state2"])
                    cp_s[h] = left(keep["corr2"])
                    dk_s[h] = keep["d_key"]

            @pl.when((done >= 0) & (done < quads))
            def _():
                ids = group_of(done)
                keeps = [
                    {"state2": halves(sp_s, h), "corr2": halves(cp_s, h), "d_key": dk_s[h]}
                    for h in ids
                ]
                together([
                    chained(adjoint_part(h, keep), last_part(h, keep))
                    for h, keep in zip(ids, keeps)
                ])
                send_edges(ids)

        @pl.when(jnp.logical_not(early))
        def _():
            due = step - lag
            forward(jnp.where(step == 0, due, -1), step, 2)
            forward(jnp.where(step == 0, -1, due), -1, 2)

            @pl.when(step < quads)
            def _():
                ids = group_of(step)
                keeps = [{} for _ in ids]
                together([adjoint_part(h, keep) for h, keep in zip(ids, keeps)])
                for h, keep in zip(ids, keeps):
                    sp_s[h] = left(keep["adj2"])
                    cp_s[h] = left(keep["dc2"])
                    yp_s[h] = left(keep["yv2"])
                    dk_s[h] = keep["d_beta"]

            @pl.when((done >= 0) & (done < quads))
            def _():
                ids = group_of(done)
                keeps = [
                    {
                        "adj2": halves(sp_s, h), "dc2": halves(cp_s, h),
                        "yv2": halves(yp_s, h), "d_beta": dk_s[h],
                    }
                    for h in ids
                ]
                together([
                    chained(state_part(h, keep), last_part(h, keep))
                    for h, keep in zip(ids, keeps)
                ])
                send_edges(ids)

        if scatter:
            @pl.when(step == 1)
            def _():
                for other in range(1, parts):
                    pl.semaphore_signal(
                        beside, inc=1, device_id=beside_of(other), device_id_type=MESH
                    )

        return carry

    lax.fori_loop(0, quads + LATE, chain, 0)

    if scatter:
        if parts > 1:
            pl.semaphore_wait(beside, parts - 1)
        piece = cgt.shape[0] // total
        cgt[...] = cg[...].T

        def cg_copy(step):
            peer, where = peer_of(step)
            return pltpu.make_async_remote_copy(
                src_ref=cgt.at[pl.ds(pl.multiple_of(peer * piece, 8), piece), :],
                dst_ref=gathered.at[step],
                send_sem=cg_send.at[step], recv_sem=cg_recv.at[step],
                device_id=where, device_id_type=MESH,
            )

        for step in range(1, total):
            cg_copy(step).start()

    @pl.when(z < shards - 1)
    def _():
        def take(h, carry):
            edge_copy(h).wait_recv()
            return carry

        lax.fori_loop(0, heads, take, 0)

    for h in range(heads):
        for s in range(3):
            lanes = slice(h * width, (h + 1) * width)
            extra = tail[h, s * 8:s * 8 + 8, :] + edge_in[h, s * 8:s * 8 + 8, :]
            grads[s][count - 8:, lanes] = extra.astype(BF16)

    if scatter:
        sums = cgt[pl.ds(pl.multiple_of(mine * piece, 8), piece), :]
        for step in range(1, total):
            cg_copy(step).wait_recv()
            sums = sums + gathered[step]
        conv_out[...] = sums
        for step in range(1, total):
            cg_copy(step).wait_send()
    else:
        conv_out[...] = cg[...]

    @pl.when(z < shards - 1)
    def _():
        halo_copy().wait_send()

        def sent(h, carry):
            state_copy(h).wait_send()
            return carry

        lax.fori_loop(0, heads, sent, 0)

    @pl.when(z > 0)
    def _():
        def sent(h, carry):
            adj_copy(h).wait_send()
            edge_copy(h).wait_send()
            return carry

        lax.fori_loop(0, heads, sent, 0)


def flush(count, *refs):
    blocks, rest = refs[:count], refs[count:]
    if len(rest) == count + 1:
        outs, sems = rest[:count], rest[count]
        extra = ()
    else:
        conv, outs, conv_out, sems, turned = rest[0], rest[1:count + 1], *rest[count + 1:]
        extra = ((turned, conv_out),)
    copies = [
        pltpu.make_async_copy(block, out, sems.at[i])
        for i, (block, out) in enumerate((*zip(blocks, outs), *extra))
    ]
    for copy in copies[:count]:
        copy.start()
    if extra:
        turned[...] = conv[...].T[:turned.shape[0]]
        copies[count].start()
    for copy in copies:
        copy.wait()


def per_device(query_raw, key_raw, value_raw, conv_weight, beta_logit, cotangent):
    shards, parts = lax.axis_size("seq"), lax.axis_size("dp")
    heads = beta_logit.shape[1]
    count, channels = query_raw.shape[1:]
    width = channels // heads
    taps = conv_weight.shape[1]
    total = shards * parts
    scatter = total > 1 and width % (8 * total) == 0
    piece = width // total if scatter else 8
    slots = total if scatter else 2
    square = lambda dtype=F32, cols=width: pltpu.VMEM((heads, count, cols), dtype)
    dma = pltpu.SemaphoreType.DMA
    vmem = pl.BlockSpec(memory_space=pltpu.VMEM)
    conv_rows = piece if scatter else width
    levels = max(1, (count // TILE - 1).bit_length())
    outs = pl.pallas_call(
        functools.partial(kernel, shards, parts, scatter),
        out_shape=(
            jax.ShapeDtypeStruct((count, channels), F32),
            jax.ShapeDtypeStruct((count, channels), BF16),
            jax.ShapeDtypeStruct((count, channels), BF16),
            jax.ShapeDtypeStruct((count, channels), BF16),
            jax.ShapeDtypeStruct((heads, count), F32),
            jax.ShapeDtypeStruct((conv_rows, 128), F32),
        ),
        in_specs=[pl.BlockSpec(memory_space=pltpu.HBM)] * 6,
        out_specs=[vmem] * 6,
        scratch_shapes=[
            pltpu.VMEM((count, channels), BF16),
            pltpu.VMEM((count, channels), BF16),
            pltpu.VMEM((count, channels), BF16),
            pltpu.VMEM((3, taps, channels), F32),
            pltpu.VMEM((heads, count), F32),
            pltpu.VMEM((count, channels), BF16),
            pltpu.VMEM((16, channels), BF16),
            pltpu.VMEM((16, channels), BF16),
            pltpu.VMEM((3, 8, channels), F32),
            square(), square(), square(),
            pltpu.VMEM((3, heads, count, width), F32),
            *[square() for _ in range(4)],
            *[square(BF16, 2 * width) for _ in range(11)],
            square(),
            pltpu.VMEM((3 * heads, count + 16, width), F32),
            pltpu.VMEM((levels, count, count), BF16),
            pltpu.VMEM((2 * count, (TILE - 1) * count), BF16),
            square(), square(),
            square(BF16), square(BF16), square(BF16), square(BF16),
            pltpu.VMEM((heads, 24, width), F32),
            pltpu.VMEM((heads, 24, width), F32),
            pltpu.VMEM((heads, 24, width), F32),
            pltpu.VMEM((128, width), F32),
            pltpu.VMEM((width, 128), F32),
            pltpu.VMEM((slots, piece, 128), F32),
            dma, dma,
            dma((heads,)), dma((heads,)), dma((heads,)), dma((heads,)),
            dma((heads,)), dma((heads,)), dma((slots,)), dma((slots,)), dma((6,)),
            pltpu.SemaphoreType.REGULAR,
        ],
        compiler_params=pltpu.CompilerParams(
            collective_id=0, has_side_effects=True, vmem_limit_bytes=48 << 20
        ),
    )(
        *(
            pltpu.with_memory_space_constraint(x, pltpu.HBM)
            for x in (
                query_raw[0], key_raw[0], value_raw[0],
                conv_weight, beta_logit[0], cotangent[0],
            )
        )
    )
    used = 3 * taps * heads
    blocks, conv = outs[:5], outs[5]
    held, free = pl.BlockSpec(memory_space=pl.ANY), pl.BlockSpec(memory_space=pltpu.HBM)
    extra_shape = (jax.ShapeDtypeStruct((used, piece), F32),) if scatter else ()
    flushed = pl.pallas_call(
        functools.partial(flush, 5),
        out_shape=(*(jax.ShapeDtypeStruct(x.shape, x.dtype) for x in blocks), *extra_shape),
        in_specs=[held] * 5 + [vmem] * len(extra_shape),
        out_specs=[free] * (5 + len(extra_shape)),
        scratch_shapes=[
            dma((5 + len(extra_shape),)),
            *(pltpu.VMEM(x.shape, F32) for x in extra_shape),
        ],
        compiler_params=pltpu.CompilerParams(vmem_limit_bytes=2 << 20),
    )(*blocks, *((conv,) if scatter else ()))
    mixed, d_query, d_key, d_value, d_beta = flushed[:5]
    if scatter:
        conv_grad = flushed[5].reshape(3, taps, heads, piece)
    else:
        conv_grad = lax.psum_scatter(
            conv[:used].reshape(3, taps, heads, width),
            ("seq", "dp"), scatter_dimension=3, tiled=True,
        )
    return (mixed[None], d_query[None], d_key[None], d_value[None], d_beta[None], conv_grad)


def solution(mesh):
    rows = P(("group", "dp"), "seq", "head")
    in_specs = (
        rows, rows, rows,
        P(None, None, "head"),
        P(("group", "dp"), "head", "seq"),
        rows,
    )
    out_specs = (
        rows, rows, rows, rows,
        P(("group", "dp"), "head", "seq"),
        P("group", None, "head", ("seq", "dp")),
    )
    return jax.shard_map(
        per_device, mesh=mesh, in_specs=in_specs, out_specs=out_specs, check_vma=False
    )
```

```python
import functools
import itertools

import jax
import jax.numpy as jnp
from jax import lax
from jax.experimental import pallas as pl
from jax.experimental.pallas import tpu as pltpu
from jax.sharding import PartitionSpec as P

MESH = pl.DeviceIdType.MESH
F32 = jnp.float32
BF16 = jnp.bfloat16
GROUP = 4
PAIR = 2
TILE = 8
RAISE = 16384.0


def pair(x):
    high = x.astype(BF16)
    return high, (x - high.astype(F32)).astype(BF16)


def left(p):
    return jnp.concatenate(p, axis=1)


def rows_of(p):
    both = jnp.concatenate(p, axis=1)
    return jnp.concatenate([both, both], axis=0)


def turned(*ps):
    return jnp.concatenate(
        [jnp.concatenate([x for p in ps for x in (p[i], p[i])], axis=1) for i in (0, 1)],
        axis=0,
    )


def flipped(p):
    return p[0].T, p[1].T


def stack(*xs):
    return jnp.concatenate(xs, axis=0)


def dot(a, b, flip=False):
    return lax.dot_general(
        a, b, (((1,), (1 if flip else 0,)), ((), ())), preferred_element_type=F32
    )


def fold(x):
    n = x.shape[1] // 2
    return x[:, :n] + x[:, n:]


def halves(ref, h):
    both = ref[h]
    n = both.shape[1] // 2
    return both[:, :n], both[:, n:]


def encode(x):
    x = x * RAISE
    square = x * x
    return (x * jnp.abs(x) * square).astype(BF16)


def decode(code):
    code = code.astype(F32)
    size = jnp.abs(code)
    root = jnp.where(size > 0.0, lax.rsqrt(lax.rsqrt(size)), 0.0) * (1.0 / RAISE)
    return jnp.where(code < 0.0, -root, root)


def kernel(
    shards, parts, scatter,
    q_hbm, k_hbm, v_hbm, conv_hbm, beta_hbm, cot_hbm,
    mixed_ref, dq_ref, dk_ref, dv_ref, dbeta_ref, conv_out,
    q_raw, k_raw, v_raw, conv_ref, beta_ref, cot_ref,
    halo_out, halo_in, before, q_s, k_s, v_s, g_s, bcol_s, pu_s, pg_s,
    kp_s, qp_s, tp_s, wp_s, up_s, rp_s, np_s, ntp_s, sp_s, cp_s, yp_s, dk_s, shift_s, masks, spread,
    loc_state, loc_adj, out_state, out_adj, in_state, in_adj,
    edge_out, edge_in, tail, cg, cgt, gathered,
    halo_send, halo_recv, state_send, state_recv, adj_send, adj_recv,
    edge_send, edge_recv, cg_send, cg_recv, load_sem, beside,
):
    z = lax.axis_index("seq")
    heads = beta_ref.shape[0]
    count, width = q_raw.shape[0], q_raw.shape[1] // heads
    first, last = z == 0, z == shards - 1
    raws = (q_raw, k_raw, v_raw)
    acts = (q_s, k_s, v_s)
    sources = (q_hbm, k_hbm, v_hbm, conv_hbm, beta_hbm, cot_hbm)
    loads = [
        pltpu.make_async_copy(source, kept, load_sem.at[i])
        for i, (source, kept) in enumerate(
            zip(sources, (q_raw, k_raw, v_raw, conv_ref, beta_ref, cot_ref))
        )
    ]
    for load in loads:
        load.start()
    grads = (dq_ref, dk_ref, dv_ref)

    barrier = pltpu.get_barrier_semaphore()
    if scatter:
        total = shards * parts
        column = lax.axis_index("dp")
        mine = z * parts + column

        def peer_of(step):
            peer = lax.rem(mine + step, total)
            return peer, {"seq": peer // parts, "dp": lax.rem(peer, parts)}

        def beside_of(step):
            return {"dp": lax.rem(column + step, parts)}

        for step in range(1, parts):
            pl.semaphore_signal(
                barrier, inc=1, device_id=beside_of(step), device_id_type=MESH
            )

    @pl.when(z > 0)
    def _():
        pl.semaphore_signal(barrier, inc=1, device_id={"seq": z - 1}, device_id_type=MESH)

    @pl.when(z < shards - 1)
    def _():
        pl.semaphore_signal(barrier, inc=1, device_id={"seq": z + 1}, device_id_type=MESH)

    met = parts - 1 if scatter else 0

    def halo_copy():
        return pltpu.make_async_remote_copy(
            src_ref=halo_out, dst_ref=halo_in,
            send_sem=halo_send, recv_sem=halo_recv,
            device_id={"seq": z + 1}, device_id_type=MESH,
        )

    def state_copy(h):
        return pltpu.make_async_remote_copy(
            src_ref=out_state.at[h], dst_ref=in_state.at[h],
            send_sem=state_send.at[h], recv_sem=state_recv.at[h],
            device_id={"seq": z + 1}, device_id_type=MESH,
        )

    def adj_copy(h):
        return pltpu.make_async_remote_copy(
            src_ref=out_adj.at[h], dst_ref=in_adj.at[h],
            send_sem=adj_send.at[h], recv_sem=adj_recv.at[h],
            device_id={"seq": z - 1}, device_id_type=MESH,
        )

    def edge_copy(h):
        return pltpu.make_async_remote_copy(
            src_ref=edge_out.at[h], dst_ref=edge_in.at[h],
            send_sem=edge_send.at[h], recv_sem=edge_recv.at[h],
            device_id={"seq": z - 1}, device_id_type=MESH,
        )

    rows = lax.broadcasted_iota(jnp.int32, (count, count), 0)
    cols = lax.broadcasted_iota(jnp.int32, (count, count), 1)
    apart = rows ^ cols
    strict = rows > cols
    lower = rows >= cols
    eye = rows == cols
    near = apart < TILE
    sizes = []
    while (TILE << len(sizes)) < count:
        sizes.append(TILE << len(sizes))
    for i, size in enumerate(sizes):
        band = (apart >= size) & (apart < 2 * size)
        masks[i] = jnp.where(band, 1.0, 0.0).astype(BF16)
    for j in range(TILE - 1):
        here = jnp.where(rows == cols - lax.rem(cols, TILE) + j, 1.0, 0.0).astype(BF16)
        spread[:, j * count:(j + 1) * count] = stack(here, here)
    cg[...] = jnp.zeros_like(cg)

    @pl.when(first)
    def _():
        in_state[...] = jnp.zeros_like(in_state)
        before[...] = jnp.zeros_like(before)

    @pl.when(last)
    def _():
        in_adj[...] = jnp.zeros_like(in_adj)
        edge_in[...] = jnp.zeros_like(edge_in)

    def lanes_of(h):
        return pl.ds(pl.multiple_of(h * width, width), width)

    for slot in range(shift_s.shape[0]):
        shift_s[slot, :8] = jnp.zeros((8, width), F32)
        shift_s[slot, 8 + count:] = jnp.zeros((8, width), F32)

    for load in loads:
        load.wait()

    @pl.when(z < shards - 1)
    def _():
        ends = [raw[count - 16:, :].astype(F32)[12:] for raw in raws]
        halo_out[...] = stack(*ends, jnp.zeros_like(ends[0])).astype(BF16)

    def activate(s, h, piece, n):
        lanes = lanes_of(h)
        taps = [conv_ref[s, j:j + 1, lanes] for j in range(4)]
        for at in range(0, n, 8):
            pre = taps[0] * piece(at + 5)
            for j in range(1, 4):
                pre = pre + taps[j] * piece(at + j + 5)
            gate = 1.0 / (1.0 + jnp.exp(-pre))
            act = pre * gate
            slope = gate * (1.0 + pre * (1.0 - gate))
            if s < 2:
                scale = lax.rsqrt(jnp.sum(act * act, axis=1, keepdims=True) + 1e-06)
                act = act * scale
                slope = slope * scale
            acts[s][h, at:at + 8] = act
            g_s[s, h, at:at + 8] = slope

    def convolve(h, carry):
        for s in range(3):
            slot = h * 3 + s
            shift_s[slot, 8:8 + count] = raws[s][:, lanes_of(h)].astype(F32)
            activate(s, h, lambda at, slot=slot: shift_s[slot, at:at + 8], count)
        row = 1.0 / (1.0 + jnp.exp(-beta_ref[pl.ds(h, 1), :]))
        column = jnp.sum(jnp.where(eye, row, 0.0), axis=1, keepdims=True)
        bcol_s[h] = jnp.broadcast_to(column, (count, width))
        return carry

    ahead = jnp.where(first, heads * 3 // 4, 0)
    lax.fori_loop(0, ahead, convolve, 0)

    @pl.when((z > 0) & (z < shards - 1))
    def _():
        pl.semaphore_wait(barrier, met + 2)

    @pl.when(first | last)
    def _():
        pl.semaphore_wait(barrier, met + 1)

    @pl.when(z < shards - 1)
    def _():
        halo_copy().start()

    lax.fori_loop(ahead, heads, convolve, 0)

    @pl.when(z > 0)
    def _():
        halo_copy().wait_recv()
        ends = halo_in[...].astype(F32)
        for s in range(3):
            three = ends[4 * s + 1:4 * s + 4]
            before[s] = stack(jnp.zeros((5, three.shape[1]), F32), three)
            for h in range(heads):
                lanes = slice(h * width, (h + 1) * width)
                ext = stack(before[s, :, lanes], raws[s][:16, lanes].astype(F32)[:8])
                activate(s, h, lambda at, ext=ext: ext[at:at + 8], 8)

    def advance(both, value):
        return value - fold(dot(both, rows_of(pair(value))))

    quads = heads // GROUP

    def pass_state(h):
        state_copy(h).wait_recv()

        @pl.when(z < shards - 1)
        def _():
            out_state[h] = encode(loc_state[h] + advance(np_s[h], decode(in_state[h])))
            state_copy(h).start()

    def pass_adjoint(h):
        adj_copy(h).wait_recv()

        @pl.when(z > 0)
        def _():
            out_adj[h] = encode(loc_adj[h] + advance(ntp_s[h], decode(in_adj[h])))
            adj_copy(h).start()

    def forward(qs, qa, least):
        def one(i, carry):
            @pl.when((qs >= 0) & (qs < quads) & (z >= least))
            def _():
                pass_state(qs * GROUP + i)

            @pl.when((qa >= 0) & (qa < quads) & (z < shards - 1))
            def _():
                pass_adjoint(qa * GROUP + i)

            return carry

        lax.fori_loop(0, GROUP, one, 0)

    def prepare(step, carry):
        ids = [step * GROUP + i for i in range(GROUP)]
        each = range(GROUP)
        qs = [q_s[h] for h in ids]
        k2 = [pair(k_s[h]) for h in ids]
        q2 = [pair(x) for x in qs]
        both = [
            fold(dot(stack(left(k), left(q)), turned(k), True)) for k, q in zip(k2, q2)
        ]
        gram = [x[:count] for x in both]
        p2 = [pair(jnp.where(lower, x[count:], 0.0)) for x in both]
        low = [jnp.where(strict, bcol_s[h] * g, 0.0) for h, g in zip(ids, gram)]
        l2 = [pair(x) for x in low]
        small = [
            jnp.sum(jnp.where(near, x, 0.0).reshape(count // TILE, TILE, count), axis=0)
            for x in low
        ]
        wide = dot(left(pair(stack(*small))), spread[...])
        lane8 = lax.rem(lax.broadcasted_iota(jnp.int32, (TILE, count), 1), TILE)
        row8 = lax.broadcasted_iota(jnp.int32, (TILE, count), 0)
        x8 = [jnp.where(lane8 == row8, 1.0, 0.0) for _ in each]
        for j in range(TILE - 1):
            x8 = [
                x - wide[i * TILE:(i + 1) * TILE, j * count:(j + 1) * count] * x[j:j + 1]
                for i, x in enumerate(x8)
            ]
        inv = [jnp.where(near, stack(*[x] * (count // TILE)), 0.0) for x in x8]
        for level in range(len(sizes)):
            mask = masks[level]
            i2 = [pair(x) for x in inv]
            part = [
                fold(dot(left(m), rows_of((a[0] * mask, a[1] * mask))))
                for m, a in zip(i2, l2)
            ]
            inv = [
                m - fold(dot(left(pair(x)), rows_of(n))) for m, x, n in zip(inv, part, i2)
            ]
        t2 = [pair(x) for x in inv]
        scaled = [
            left(pair(m * (1.0 / (1.0 + jnp.exp(-beta_ref[pl.ds(h, 1), :])))))
            for h, m in zip(ids, inv)
        ]
        w2 = [pair(fold(dot(t, rows_of(k)))) for t, k in zip(scaled, k2)]
        u2 = [pair(fold(dot(t, rows_of(pair(v_s[h]))))) for h, t in zip(ids, scaled)]
        onto = [stack(left(flipped(k)), left(p)) for k, p in zip(k2, p2)]
        on_w = [fold(dot(a, rows_of(w))) for a, w in zip(onto, w2)]
        on_u = [fold(dot(a, rows_of(u))) for a, u in zip(onto, u2)]
        r2 = [pair(q - x[count:]) for q, x in zip(qs, on_w)]
        n2 = [pair(x[:width]) for x in on_w]
        cots = [cot_ref[:, lanes_of(h)] for h in ids]
        back = [
            dot(stack(left(flipped(r)), left(flipped(p))), stack(c, c))
            for r, p, c in zip(r2, p2, cots)
        ]

        @pl.when(first)
        def _():
            for i, h in enumerate(ids):
                out_state[h] = encode(on_u[i][:width])
                state_copy(h).start()

        @pl.when(last)
        def _():
            for i, h in enumerate(ids):
                out_adj[h] = encode(back[i][:width])
                adj_copy(h).start()

        for i, h in enumerate(ids):
            loc_state[h] = on_u[i][:width]
            loc_adj[h] = back[i][:width]
            pu_s[h] = on_u[i][width:]
            pg_s[h] = back[i][width:]
            kp_s[h] = left(k2[i])
            qp_s[h] = left(q2[i])
            tp_s[h] = left(flipped(t2[i]))
            wp_s[h] = left(w2[i])
            up_s[h] = left(u2[i])
            rp_s[h] = left(r2[i])
            np_s[h] = left(n2[i])
            ntp_s[h] = left(flipped(n2[i]))

        @pl.when(z == 1)
        def _():
            forward(step, -1, 1)

        return carry

    lax.fori_loop(0, heads // GROUP, prepare, 0)

    def conv_back(s, h, grad):
        lanes, slot = lanes_of(h), h * 3 + s
        if s < 2:
            unit = acts[s][h]
            grad = grad - unit * jnp.sum(grad * unit, axis=1, keepdims=True)
        shift_s[slot, 8:8 + count] = grad * g_s[s, h]
        yield
        taps = [conv_ref[s, j:j + 1, lanes] for j in range(4)]
        sums = [None] * 4
        for at in range(0, count + 8, 8):
            if at == 0:
                series = before[s, :, lanes]
            elif at % 16 == 8:
                both = raws[s][at - 8:at + 8, lanes].astype(F32)
                series = both[:8]
            else:
                series = both[8:]
            full = None
            for j in range(4):
                moved = shift_s[slot, at + 3 - j:at + 11 - j]
                term, product = taps[j] * moved, series * moved
                full = term if full is None else full + term
                sums[j] = product if sums[j] is None else sums[j] + product
            if at == 0:
                edge_out[h, s * 8:s * 8 + 8, :] = full
            elif at % 16 == 8:
                held = full
            else:
                grads[s][at - 16:at, lanes] = stack(held, full).astype(BF16)
        tail[h, s * 8:s * 8 + 8, :] = full
        for j in range(4):
            cg[pl.ds((s * 4 + j) * heads + h, 1), :] = jnp.sum(sums[j], axis=0, keepdims=True)

    def state_part(h, keep):
        lanes = lanes_of(h)
        cot = cot_ref[:, lanes]
        state2 = pair(decode(in_state[h]))
        k2, q2, u2 = (halves(x, h) for x in (kp_s, qp_s, up_s))
        reads = fold(dot(stack(wp_s[h], rp_s[h]), rows_of(state2)))
        d_query = fold(dot(cot, stack(*state2), True))
        yield
        mixed_ref[:, lanes] = reads[count:] + pu_s[h]
        corr2 = pair((u2[0].astype(F32) - reads[:count]) + u2[1].astype(F32))
        yield
        ds2 = pair(jnp.where(lower, fold(dot(cot, stack(*corr2), True)), 0.0))
        yield
        d_query = d_query + fold(dot(left(ds2), rows_of(k2)))
        d_key = fold(dot(left(flipped(ds2)), rows_of(q2)))
        keep.update(state2=state2, corr2=corr2, d_key=d_key)
        yield
        yield from conv_back(0, h, d_query)

    def adjoint_part(h, keep):
        adj2 = pair(decode(in_adj[h]))
        dc2 = pair(pg_s[h] + fold(dot(kp_s[h], rows_of(adj2))))
        yield
        y_v = fold(dot(tp_s[h], rows_of(dc2)))
        keep.update(adj2=adj2, yv2=pair(y_v))
        yield
        yield from conv_back(2, h, bcol_s[h] * y_v)

    def last_part(h, keep):
        corr2, yv2 = keep["corr2"], keep["yv2"]
        ys = left(yv2)
        d_gram = jnp.where(strict, -bcol_s[h] * fold(dot(ys, turned(corr2), True)), 0.0)
        y_k = -fold(dot(ys, turned(keep["state2"]), True))
        yield
        d_key = (
            keep["d_key"] + bcol_s[h] * y_k
            + fold(dot(left(corr2), turned(keep["adj2"]), True))
            + fold(dot(left(pair(d_gram + d_gram.T)), rows_of(halves(kp_s, h))))
        )
        yield
        inner = sum(x.astype(F32) for x in yv2) * sum(x.astype(F32) for x in corr2)
        column = jnp.sum(inner, axis=1, keepdims=True)
        row = jnp.sum(jnp.where(eye, column, 0.0), axis=0, keepdims=True)
        dbeta_ref[pl.ds(h, 1), :] = row / (1.0 + jnp.exp(beta_ref[pl.ds(h, 1), :]))
        yield from conv_back(1, h, d_key)

    def together(gens):
        for _ in itertools.zip_longest(*gens):
            pass

    def chained(*gens):
        for gen in gens:
            yield from gen

    early = z < shards // 2

    def group_of(q):
        return [q * GROUP + i for i in range(GROUP)]

    def send_edges(ids):
        @pl.when(z > 0)
        def _():
            for h in ids:
                edge_copy(h).start()

    def chain(step, carry):
        ids = group_of(step)
        keeps = [{} for _ in ids]

        @pl.when(early)
        def _():
            forward(step, jnp.where(first, -1, step - 1), 2)
            together([state_part(h, keep) for h, keep in zip(ids, keeps)])
            for h, keep in zip(ids, keeps):
                sp_s[h] = left(keep["state2"])
                cp_s[h] = left(keep["corr2"])
                dk_s[h] = keep["d_key"]

        @pl.when(jnp.logical_not(early))
        def _():
            forward(-1, step, 2)
            forward(jnp.where(last, -1, step), -1, 2)
            together([adjoint_part(h, keep) for h, keep in zip(ids, keeps)])
            for h, keep in zip(ids, keeps):
                sp_s[h] = left(keep["adj2"])
                yp_s[h] = left(keep["yv2"])

        if scatter:
            @pl.when(step == 1)
            def _():
                for other in range(1, parts):
                    pl.semaphore_signal(
                        beside, inc=1, device_id=beside_of(other), device_id_type=MESH
                    )

        return carry

    lax.fori_loop(0, quads, chain, 0)

    @pl.when(early & (z > 0))
    def _():
        forward(-1, quads - 1, 2)

    def complete(step, carry):
        ids = [step * PAIR + i for i in range(PAIR)]

        @pl.when(first & (z < shards - 1))
        def _():
            for h in ids:
                adj_copy(h).wait_recv()

        @pl.when(last & (z > 1))
        def _():
            for h in ids:
                state_copy(h).wait_recv()

        @pl.when(early)
        def _():
            keeps = [
                {"state2": halves(sp_s, h), "corr2": halves(cp_s, h), "d_key": dk_s[h]}
                for h in ids
            ]
            together([
                chained(adjoint_part(h, keep), last_part(h, keep))
                for h, keep in zip(ids, keeps)
            ])

        @pl.when(jnp.logical_not(early))
        def _():
            keeps = [{"adj2": halves(sp_s, h), "yv2": halves(yp_s, h)} for h in ids]
            together([
                chained(state_part(h, keep), last_part(h, keep))
                for h, keep in zip(ids, keeps)
            ])

        send_edges(ids)
        return carry

    lax.fori_loop(0, heads // PAIR, complete, 0)

    if scatter:
        if parts > 1:
            pl.semaphore_wait(beside, parts - 1)
        piece = cgt.shape[0] // total
        cgt[...] = cg[...].T

        def cg_copy(step):
            peer, where = peer_of(step)
            return pltpu.make_async_remote_copy(
                src_ref=cgt.at[pl.ds(pl.multiple_of(peer * piece, 8), piece), :],
                dst_ref=gathered.at[step],
                send_sem=cg_send.at[step], recv_sem=cg_recv.at[step],
                device_id=where, device_id_type=MESH,
            )

        for step in range(1, total):
            cg_copy(step).start()

    @pl.when(z < shards - 1)
    def _():
        def take(h, carry):
            edge_copy(h).wait_recv()
            return carry

        lax.fori_loop(0, heads, take, 0)

    for h in range(heads):
        for s in range(3):
            lanes = slice(h * width, (h + 1) * width)
            extra = tail[h, s * 8:s * 8 + 8, :] + edge_in[h, s * 8:s * 8 + 8, :]
            grads[s][count - 8:, lanes] = extra.astype(BF16)

    @pl.when(z < shards - 1)
    def _():
        halo_copy().wait_send()

        def sent(h, carry):
            state_copy(h).wait_send()
            return carry

        lax.fori_loop(0, heads, sent, 0)

    @pl.when(z > 0)
    def _():
        def sent(h, carry):
            adj_copy(h).wait_send()
            edge_copy(h).wait_send()
            return carry

        lax.fori_loop(0, heads, sent, 0)

    if scatter:
        sums = cgt[pl.ds(pl.multiple_of(mine * piece, 8), piece), :]
        for step in range(1, total):
            cg_copy(step).wait_recv()
            sums = sums + gathered[step]
        conv_out[...] = sums
        for step in range(1, total):
            cg_copy(step).wait_send()
    else:
        conv_out[...] = cg[...]


def flush(count, *refs):
    blocks, rest = refs[:count], refs[count:]
    if len(rest) == count + 1:
        outs, sems = rest[:count], rest[count]
        extra = ()
    else:
        conv, outs, conv_out, sems, turned = rest[0], rest[1:count + 1], *rest[count + 1:]
        extra = ((turned, conv_out),)
    copies = [
        pltpu.make_async_copy(block, out, sems.at[i])
        for i, (block, out) in enumerate((*zip(blocks, outs), *extra))
    ]
    for copy in copies[:count]:
        copy.start()
    if extra:
        turned[...] = conv[...].T[:turned.shape[0]]
        copies[count].start()
    for copy in copies:
        copy.wait()


def per_device(query_raw, key_raw, value_raw, conv_weight, beta_logit, cotangent):
    shards, parts = lax.axis_size("seq"), lax.axis_size("dp")
    heads = beta_logit.shape[1]
    count, channels = query_raw.shape[1:]
    width = channels // heads
    taps = conv_weight.shape[1]
    total = shards * parts
    scatter = total > 1 and width % (8 * total) == 0
    piece = width // total if scatter else 8
    slots = total if scatter else 2
    square = lambda dtype=F32, cols=width: pltpu.VMEM((heads, count, cols), dtype)
    dma = pltpu.SemaphoreType.DMA
    vmem = pl.BlockSpec(memory_space=pltpu.VMEM)
    conv_rows = piece if scatter else width
    levels = max(1, (count // TILE - 1).bit_length())
    outs = pl.pallas_call(
        functools.partial(kernel, shards, parts, scatter),
        out_shape=(
            jax.ShapeDtypeStruct((count, channels), F32),
            jax.ShapeDtypeStruct((count, channels), BF16),
            jax.ShapeDtypeStruct((count, channels), BF16),
            jax.ShapeDtypeStruct((count, channels), BF16),
            jax.ShapeDtypeStruct((heads, count), F32),
            jax.ShapeDtypeStruct((conv_rows, 128), F32),
        ),
        in_specs=[pl.BlockSpec(memory_space=pltpu.HBM)] * 6,
        out_specs=[vmem] * 6,
        scratch_shapes=[
            pltpu.VMEM((count, channels), BF16),
            pltpu.VMEM((count, channels), BF16),
            pltpu.VMEM((count, channels), BF16),
            pltpu.VMEM((3, taps, channels), F32),
            pltpu.VMEM((heads, count), F32),
            pltpu.VMEM((count, channels), BF16),
            pltpu.VMEM((16, channels), BF16),
            pltpu.VMEM((16, channels), BF16),
            pltpu.VMEM((3, 8, channels), F32),
            square(), square(), square(),
            pltpu.VMEM((3, heads, count, width), F32),
            *[square() for _ in range(3)],
            *[square(BF16, 2 * width) for _ in range(11)],
            square(),
            pltpu.VMEM((3 * heads, count + 16, width), F32),
            pltpu.VMEM((levels, count, count), BF16),
            pltpu.VMEM((2 * count, (TILE - 1) * count), BF16),
            square(), square(),
            square(BF16), square(BF16), square(BF16), square(BF16),
            pltpu.VMEM((heads, 24, width), F32),
            pltpu.VMEM((heads, 24, width), F32),
            pltpu.VMEM((heads, 24, width), F32),
            pltpu.VMEM((128, width), F32),
            pltpu.VMEM((width, 128), F32),
            pltpu.VMEM((slots, piece, 128), F32),
            dma, dma,
            dma((heads,)), dma((heads,)), dma((heads,)), dma((heads,)),
            dma((heads,)), dma((heads,)), dma((slots,)), dma((slots,)), dma((6,)),
            pltpu.SemaphoreType.REGULAR,
        ],
        compiler_params=pltpu.CompilerParams(
            collective_id=0, has_side_effects=True, vmem_limit_bytes=48 << 20
        ),
    )(
        *(
            pltpu.with_memory_space_constraint(x, pltpu.HBM)
            for x in (
                query_raw[0], key_raw[0], value_raw[0],
                conv_weight, beta_logit[0], cotangent[0],
            )
        )
    )
    used = 3 * taps * heads
    blocks, conv = outs[:5], outs[5]
    held, free = pl.BlockSpec(memory_space=pl.ANY), pl.BlockSpec(memory_space=pltpu.HBM)
    extra_shape = (jax.ShapeDtypeStruct((used, piece), F32),) if scatter else ()
    flushed = pl.pallas_call(
        functools.partial(flush, 5),
        out_shape=(*(jax.ShapeDtypeStruct(x.shape, x.dtype) for x in blocks), *extra_shape),
        in_specs=[held] * 5 + [vmem] * len(extra_shape),
        out_specs=[free] * (5 + len(extra_shape)),
        scratch_shapes=[
            dma((5 + len(extra_shape),)),
            *(pltpu.VMEM(x.shape, F32) for x in extra_shape),
        ],
        compiler_params=pltpu.CompilerParams(vmem_limit_bytes=2 << 20),
    )(*blocks, *((conv,) if scatter else ()))
    mixed, d_query, d_key, d_value, d_beta = flushed[:5]
    if scatter:
        conv_grad = flushed[5].reshape(3, taps, heads, piece)
    else:
        conv_grad = lax.psum_scatter(
            conv[:used].reshape(3, taps, heads, width),
            ("seq", "dp"), scatter_dimension=3, tiled=True,
        )
    return (mixed[None], d_query[None], d_key[None], d_value[None], d_beta[None], conv_grad)


def solution(mesh):
    rows = P(("group", "dp"), "seq", "head")
    in_specs = (
        rows, rows, rows,
        P(None, None, "head"),
        P(("group", "dp"), "head", "seq"),
        rows,
    )
    out_specs = (
        rows, rows, rows, rows,
        P(("group", "dp"), "head", "seq"),
        P("group", None, "head", ("seq", "dp")),
    )
    return jax.shard_map(
        per_device, mesh=mesh, in_specs=in_specs, out_specs=out_specs, check_vma=False
    )
```

```python
import functools
import itertools

import jax
import jax.numpy as jnp
from jax import lax
from jax.experimental import pallas as pl
from jax.experimental.pallas import tpu as pltpu
from jax.sharding import PartitionSpec as P

MESH = pl.DeviceIdType.MESH
F32 = jnp.float32
BF16 = jnp.bfloat16
GROUP = 4
PAIR = 2
TILE = 16
RAISE = 16384.0


def pair(x):
    high = x.astype(BF16)
    return high, (x - high.astype(F32)).astype(BF16)


def left(p):
    return jnp.concatenate(p, axis=1)


def rows_of(p):
    both = jnp.concatenate(p, axis=1)
    return jnp.concatenate([both, both], axis=0)


def turned(*ps):
    return jnp.concatenate(
        [jnp.concatenate([x for p in ps for x in (p[i], p[i])], axis=1) for i in (0, 1)],
        axis=0,
    )


def flipped(p):
    return p[0].T, p[1].T


def stack(*xs):
    return jnp.concatenate(xs, axis=0)


def dot(a, b, flip=False):
    return lax.dot_general(
        a, b, (((1,), (1 if flip else 0,)), ((), ())), preferred_element_type=F32
    )


def fold(x):
    n = x.shape[1] // 2
    return x[:, :n] + x[:, n:]


def halves(ref, h):
    both = ref[h]
    n = both.shape[1] // 2
    return both[:, :n], both[:, n:]


def encode(x):
    x = x * RAISE
    square = x * x
    return (x * jnp.abs(x) * square).astype(BF16)


def decode(code):
    code = code.astype(F32)
    size = jnp.abs(code)
    root = jnp.where(size > 0.0, lax.rsqrt(lax.rsqrt(size)), 0.0) * (1.0 / RAISE)
    return jnp.where(code < 0.0, -root, root)


def kernel(
    shards, parts, scatter,
    q_hbm, k_hbm, v_hbm, conv_hbm, beta_hbm, cot_hbm,
    mixed_ref, dq_ref, dk_ref, dv_ref, dbeta_ref, conv_out,
    q_raw, k_raw, v_raw, conv_ref, beta_ref, cot_ref,
    halo_out, halo_in, before, q_s, k_s, v_s, g_s, bcol_s, pu_s, pg_s,
    kp_s, qp_s, tp_s, wp_s, up_s, rp_s, np_s, ntp_s, sp_s, cp_s, yp_s, dk_s, shift_s, masks,
    loc_state, loc_adj, out_state, out_adj, in_state, in_adj,
    edge_out, edge_in, tail, cg, cgt, gathered,
    halo_send, halo_recv, state_send, state_recv, adj_send, adj_recv,
    edge_send, edge_recv, cg_send, cg_recv, load_sem, beside,
):
    z = lax.axis_index("seq")
    heads = beta_ref.shape[0]
    count, width = q_raw.shape[0], q_raw.shape[1] // heads
    first, last = z == 0, z == shards - 1
    raws = (q_raw, k_raw, v_raw)
    acts = (q_s, k_s, v_s)
    sources = (q_hbm, k_hbm, v_hbm, conv_hbm, beta_hbm, cot_hbm)
    loads = [
        pltpu.make_async_copy(source, kept, load_sem.at[i])
        for i, (source, kept) in enumerate(
            zip(sources, (q_raw, k_raw, v_raw, conv_ref, beta_ref, cot_ref))
        )
    ]
    for load in loads:
        load.start()
    grads = (dq_ref, dk_ref, dv_ref)

    barrier = pltpu.get_barrier_semaphore()
    if scatter:
        total = shards * parts
        column = lax.axis_index("dp")
        mine = z * parts + column

        def peer_of(step):
            peer = lax.rem(mine + step, total)
            return peer, {"seq": peer // parts, "dp": lax.rem(peer, parts)}

        def beside_of(step):
            return {"dp": lax.rem(column + step, parts)}

        for step in range(1, parts):
            pl.semaphore_signal(
                barrier, inc=1, device_id=beside_of(step), device_id_type=MESH
            )

    @pl.when(z > 0)
    def _():
        pl.semaphore_signal(barrier, inc=1, device_id={"seq": z - 1}, device_id_type=MESH)

    @pl.when(z < shards - 1)
    def _():
        pl.semaphore_signal(barrier, inc=1, device_id={"seq": z + 1}, device_id_type=MESH)

    met = parts - 1 if scatter else 0

    def halo_copy():
        return pltpu.make_async_remote_copy(
            src_ref=halo_out, dst_ref=halo_in,
            send_sem=halo_send, recv_sem=halo_recv,
            device_id={"seq": z + 1}, device_id_type=MESH,
        )

    def state_copy(h):
        return pltpu.make_async_remote_copy(
            src_ref=out_state.at[h], dst_ref=in_state.at[h],
            send_sem=state_send.at[h], recv_sem=state_recv.at[h],
            device_id={"seq": z + 1}, device_id_type=MESH,
        )

    def adj_copy(h):
        return pltpu.make_async_remote_copy(
            src_ref=out_adj.at[h], dst_ref=in_adj.at[h],
            send_sem=adj_send.at[h], recv_sem=adj_recv.at[h],
            device_id={"seq": z - 1}, device_id_type=MESH,
        )

    def edge_copy(h):
        return pltpu.make_async_remote_copy(
            src_ref=edge_out.at[h], dst_ref=edge_in.at[h],
            send_sem=edge_send.at[h], recv_sem=edge_recv.at[h],
            device_id={"seq": z - 1}, device_id_type=MESH,
        )

    rows = lax.broadcasted_iota(jnp.int32, (count, count), 0)
    cols = lax.broadcasted_iota(jnp.int32, (count, count), 1)
    apart = rows ^ cols
    strict = rows > cols
    lower = rows >= cols
    eye = rows == cols
    near = apart < TILE
    sizes = []
    while (TILE << len(sizes)) < count:
        sizes.append(TILE << len(sizes))
    for i, size in enumerate(sizes):
        band = (apart >= size) & (apart < 2 * size)
        masks[i] = jnp.where(band, 1.0, 0.0).astype(BF16)
    cg[...] = jnp.zeros_like(cg)

    @pl.when(first)
    def _():
        in_state[...] = jnp.zeros_like(in_state)
        before[...] = jnp.zeros_like(before)

    @pl.when(last)
    def _():
        in_adj[...] = jnp.zeros_like(in_adj)
        edge_in[...] = jnp.zeros_like(edge_in)

    def lanes_of(h):
        return pl.ds(pl.multiple_of(h * width, width), width)

    for slot in range(shift_s.shape[0]):
        shift_s[slot, :8] = jnp.zeros((8, width), F32)
        shift_s[slot, 8 + count:] = jnp.zeros((8, width), F32)

    for load in loads:
        load.wait()

    @pl.when(z < shards - 1)
    def _():
        ends = [raw[count - 16:, :].astype(F32)[12:] for raw in raws]
        halo_out[...] = stack(*ends, jnp.zeros_like(ends[0])).astype(BF16)

    def activate(s, h, piece, n):
        lanes = lanes_of(h)
        taps = [conv_ref[s, j:j + 1, lanes] for j in range(4)]
        for at in range(0, n, 8):
            pre = taps[0] * piece(at + 5)
            for j in range(1, 4):
                pre = pre + taps[j] * piece(at + j + 5)
            gate = 1.0 / (1.0 + jnp.exp(-pre))
            act = pre * gate
            slope = gate * (1.0 + pre * (1.0 - gate))
            if s < 2:
                scale = lax.rsqrt(jnp.sum(act * act, axis=1, keepdims=True) + 1e-06)
                act = act * scale
                slope = slope * scale
            acts[s][h, at:at + 8] = act
            g_s[s, h, at:at + 8] = slope

    def convolve(h, carry):
        for s in range(3):
            slot = h * 3 + s
            shift_s[slot, 8:8 + count] = raws[s][:, lanes_of(h)].astype(F32)
            activate(s, h, lambda at, slot=slot: shift_s[slot, at:at + 8], count)
        row = 1.0 / (1.0 + jnp.exp(-beta_ref[pl.ds(h, 1), :]))
        column = jnp.sum(jnp.where(eye, row, 0.0), axis=1, keepdims=True)
        bcol_s[h] = jnp.broadcast_to(column, (count, width))
        return carry

    ahead = jnp.where(first, heads * 3 // 4, 0)
    lax.fori_loop(0, ahead, convolve, 0)

    @pl.when((z > 0) & (z < shards - 1))
    def _():
        pl.semaphore_wait(barrier, met + 2)

    @pl.when(first | last)
    def _():
        pl.semaphore_wait(barrier, met + 1)

    @pl.when(z < shards - 1)
    def _():
        halo_copy().start()

    lax.fori_loop(ahead, heads, convolve, 0)

    @pl.when(z > 0)
    def _():
        halo_copy().wait_recv()
        ends = halo_in[...].astype(F32)
        for s in range(3):
            three = ends[4 * s + 1:4 * s + 4]
            before[s] = stack(jnp.zeros((5, three.shape[1]), F32), three)
            for h in range(heads):
                lanes = slice(h * width, (h + 1) * width)
                ext = stack(before[s, :, lanes], raws[s][:16, lanes].astype(F32)[:8])
                activate(s, h, lambda at, ext=ext: ext[at:at + 8], 8)

    def advance(both, value):
        return value - fold(dot(both, rows_of(pair(value))))

    quads = heads // GROUP

    def pass_state(h):
        state_copy(h).wait_recv()

        @pl.when(z < shards - 1)
        def _():
            out_state[h] = encode(loc_state[h] + advance(np_s[h], decode(in_state[h])))
            state_copy(h).start()

    def pass_adjoint(h):
        adj_copy(h).wait_recv()

        @pl.when(z > 0)
        def _():
            out_adj[h] = encode(loc_adj[h] + advance(ntp_s[h], decode(in_adj[h])))
            adj_copy(h).start()

    def forward(qs, qa, least):
        def one(i, carry):
            @pl.when((qs >= 0) & (qs < quads) & (z >= least))
            def _():
                pass_state(qs * GROUP + i)

            @pl.when((qa >= 0) & (qa < quads) & (z < shards - 1))
            def _():
                pass_adjoint(qa * GROUP + i)

            return carry

        lax.fori_loop(0, GROUP, one, 0)

    def prepare(step, carry):
        ids = [step * GROUP + i for i in range(GROUP)]
        each = range(GROUP)
        qs = [q_s[h] for h in ids]
        k2 = [pair(k_s[h]) for h in ids]
        q2 = [pair(x) for x in qs]
        both = [
            fold(dot(stack(left(k), left(q)), turned(k), True)) for k, q in zip(k2, q2)
        ]
        gram = [x[:count] for x in both]
        p2 = [pair(jnp.where(lower, x[count:], 0.0)) for x in both]
        low = [jnp.where(strict, bcol_s[h] * g, 0.0) for h, g in zip(ids, gram)]
        l2 = [pair(x) for x in low]
        small = [
            jnp.sum(jnp.where(near, x, 0.0).reshape(count // TILE, TILE, count), axis=0)
            for x in low
        ]
        lane = lax.broadcasted_iota(jnp.int32, (8, count), 1)
        base = lane - lax.rem(lane, TILE)
        row8 = lax.broadcasted_iota(jnp.int32, (8, count), 0)
        parts8 = TILE // 8
        x8 = [
            [jnp.where(lane - base == row8 + 8 * p, 1.0, 0.0) for p in range(parts8)]
            for _ in each
        ]
        for j in range(TILE - 1):
            for x, m in zip(x8, small):
                pivot = x[j // 8][j % 8:j % 8 + 1]
                for p in range(j // 8, parts8):
                    column = jnp.take_along_axis(
                        m[8 * p:8 * p + 8], base + j, axis=1, mode="promise_in_bounds"
                    )
                    x[p] = x[p] - column * pivot
        x8 = [stack(*x) for x in x8]
        inv = [jnp.where(near, stack(*[x] * (count // TILE)), 0.0) for x in x8]
        for level in range(len(sizes)):
            mask = masks[level]
            i2 = [pair(x) for x in inv]
            part = [
                fold(dot(left(m), rows_of((a[0] * mask, a[1] * mask))))
                for m, a in zip(i2, l2)
            ]
            inv = [
                m - fold(dot(left(pair(x)), rows_of(n))) for m, x, n in zip(inv, part, i2)
            ]
        t2 = [pair(x) for x in inv]
        scaled = [
            left(pair(m * (1.0 / (1.0 + jnp.exp(-beta_ref[pl.ds(h, 1), :])))))
            for h, m in zip(ids, inv)
        ]
        w2 = [pair(fold(dot(t, rows_of(k)))) for t, k in zip(scaled, k2)]
        u2 = [pair(fold(dot(t, rows_of(pair(v_s[h]))))) for h, t in zip(ids, scaled)]
        onto = [stack(left(flipped(k)), left(p)) for k, p in zip(k2, p2)]
        on_w = [fold(dot(a, rows_of(w))) for a, w in zip(onto, w2)]
        on_u = [fold(dot(a, rows_of(u))) for a, u in zip(onto, u2)]
        r2 = [pair(q - x[count:]) for q, x in zip(qs, on_w)]
        n2 = [pair(x[:width]) for x in on_w]
        cots = [cot_ref[:, lanes_of(h)] for h in ids]
        back = [
            dot(stack(left(flipped(r)), left(flipped(p))), stack(c, c))
            for r, p, c in zip(r2, p2, cots)
        ]

        @pl.when(first)
        def _():
            for i, h in enumerate(ids):
                out_state[h] = encode(on_u[i][:width])
                state_copy(h).start()

        @pl.when(last)
        def _():
            for i, h in enumerate(ids):
                out_adj[h] = encode(back[i][:width])
                adj_copy(h).start()

        for i, h in enumerate(ids):
            loc_state[h] = on_u[i][:width]
            loc_adj[h] = back[i][:width]
            pu_s[h] = on_u[i][width:]
            pg_s[h] = back[i][width:]
            kp_s[h] = left(k2[i])
            qp_s[h] = left(q2[i])
            tp_s[h] = left(flipped(t2[i]))
            wp_s[h] = left(w2[i])
            up_s[h] = left(u2[i])
            rp_s[h] = left(r2[i])
            np_s[h] = left(n2[i])
            ntp_s[h] = left(flipped(n2[i]))

        @pl.when(z == 1)
        def _():
            forward(step, -1, 1)

        return carry

    lax.fori_loop(0, heads // GROUP, prepare, 0)

    def conv_back(s, h, grad):
        lanes, slot = lanes_of(h), h * 3 + s
        if s < 2:
            unit = acts[s][h]
            grad = grad - unit * jnp.sum(grad * unit, axis=1, keepdims=True)
        shift_s[slot, 8:8 + count] = grad * g_s[s, h]
        yield
        taps = [conv_ref[s, j:j + 1, lanes] for j in range(4)]
        sums = [None] * 4
        for at in range(0, count + 8, 8):
            if at == 0:
                series = before[s, :, lanes]
            elif at % 16 == 8:
                both = raws[s][at - 8:at + 8, lanes].astype(F32)
                series = both[:8]
            else:
                series = both[8:]
            full = None
            for j in range(4):
                moved = shift_s[slot, at + 3 - j:at + 11 - j]
                term, product = taps[j] * moved, series * moved
                full = term if full is None else full + term
                sums[j] = product if sums[j] is None else sums[j] + product
            if at == 0:
                edge_out[h, s * 8:s * 8 + 8, :] = full
            elif at % 16 == 8:
                held = full
            else:
                grads[s][at - 16:at, lanes] = stack(held, full).astype(BF16)
        tail[h, s * 8:s * 8 + 8, :] = full
        for j in range(4):
            cg[pl.ds((s * 4 + j) * heads + h, 1), :] = jnp.sum(sums[j], axis=0, keepdims=True)

    def state_part(h, keep):
        lanes = lanes_of(h)
        cot = cot_ref[:, lanes]
        state2 = pair(decode(in_state[h]))
        k2, q2, u2 = (halves(x, h) for x in (kp_s, qp_s, up_s))
        reads = fold(dot(stack(wp_s[h], rp_s[h]), rows_of(state2)))
        d_query = fold(dot(cot, stack(*state2), True))
        yield
        mixed_ref[:, lanes] = reads[count:] + pu_s[h]
        corr2 = pair((u2[0].astype(F32) - reads[:count]) + u2[1].astype(F32))
        yield
        ds2 = pair(jnp.where(lower, fold(dot(cot, stack(*corr2), True)), 0.0))
        yield
        d_query = d_query + fold(dot(left(ds2), rows_of(k2)))
        d_key = fold(dot(left(flipped(ds2)), rows_of(q2)))
        keep.update(state2=state2, corr2=corr2, d_key=d_key)
        yield
        yield from conv_back(0, h, d_query)

    def adjoint_part(h, keep):
        adj2 = pair(decode(in_adj[h]))
        dc2 = pair(pg_s[h] + fold(dot(kp_s[h], rows_of(adj2))))
        yield
        y_v = fold(dot(tp_s[h], rows_of(dc2)))
        keep.update(adj2=adj2, yv2=pair(y_v))
        yield
        yield from conv_back(2, h, bcol_s[h] * y_v)

    def last_part(h, keep):
        corr2, yv2 = keep["corr2"], keep["yv2"]
        ys = left(yv2)
        d_gram = jnp.where(strict, -bcol_s[h] * fold(dot(ys, turned(corr2), True)), 0.0)
        y_k = -fold(dot(ys, turned(keep["state2"]), True))
        yield
        d_key = (
            keep["d_key"] + bcol_s[h] * y_k
            + fold(dot(left(corr2), turned(keep["adj2"]), True))
            + fold(dot(left(pair(d_gram + d_gram.T)), rows_of(halves(kp_s, h))))
        )
        yield
        inner = sum(x.astype(F32) for x in yv2) * sum(x.astype(F32) for x in corr2)
        column = jnp.sum(inner, axis=1, keepdims=True)
        row = jnp.sum(jnp.where(eye, column, 0.0), axis=0, keepdims=True)
        dbeta_ref[pl.ds(h, 1), :] = row / (1.0 + jnp.exp(beta_ref[pl.ds(h, 1), :]))
        yield from conv_back(1, h, d_key)

    def together(gens):
        for _ in itertools.zip_longest(*gens):
            pass

    def chained(*gens):
        for gen in gens:
            yield from gen

    early = z < shards // 2

    def group_of(q):
        return [q * GROUP + i for i in range(GROUP)]

    def send_edges(ids):
        @pl.when(z > 0)
        def _():
            for h in ids:
                edge_copy(h).start()

    def chain(step, carry):
        ids = group_of(step)
        keeps = [{} for _ in ids]

        @pl.when(early)
        def _():
            forward(step, jnp.where(first, -1, step - 1), 2)
            together([state_part(h, keep) for h, keep in zip(ids, keeps)])
            for h, keep in zip(ids, keeps):
                sp_s[h] = left(keep["state2"])
                cp_s[h] = left(keep["corr2"])
                dk_s[h] = keep["d_key"]

        @pl.when(jnp.logical_not(early))
        def _():
            forward(-1, step, 2)
            forward(jnp.where(last, -1, step), -1, 2)
            together([adjoint_part(h, keep) for h, keep in zip(ids, keeps)])
            for h, keep in zip(ids, keeps):
                sp_s[h] = left(keep["adj2"])
                yp_s[h] = left(keep["yv2"])

        if scatter:
            @pl.when(step == 1)
            def _():
                for other in range(1, parts):
                    pl.semaphore_signal(
                        beside, inc=1, device_id=beside_of(other), device_id_type=MESH
                    )

        return carry

    lax.fori_loop(0, quads, chain, 0)

    @pl.when(early & (z > 0))
    def _():
        forward(-1, quads - 1, 2)

    def complete(step, carry):
        ids = [step * PAIR + i for i in range(PAIR)]

        @pl.when(first & (z < shards - 1))
        def _():
            for h in ids:
                adj_copy(h).wait_recv()

        @pl.when(last & (z > 1))
        def _():
            for h in ids:
                state_copy(h).wait_recv()

        @pl.when(early)
        def _():
            keeps = [
                {"state2": halves(sp_s, h), "corr2": halves(cp_s, h), "d_key": dk_s[h]}
                for h in ids
            ]
            together([
                chained(adjoint_part(h, keep), last_part(h, keep))
                for h, keep in zip(ids, keeps)
            ])

        @pl.when(jnp.logical_not(early))
        def _():
            keeps = [{"adj2": halves(sp_s, h), "yv2": halves(yp_s, h)} for h in ids]
            together([
                chained(state_part(h, keep), last_part(h, keep))
                for h, keep in zip(ids, keeps)
            ])

        send_edges(ids)
        return carry

    lax.fori_loop(0, heads // PAIR, complete, 0)

    if scatter:
        if parts > 1:
            pl.semaphore_wait(beside, parts - 1)
        piece = cgt.shape[0] // total
        cgt[...] = cg[...].T

        def cg_copy(step):
            peer, where = peer_of(step)
            return pltpu.make_async_remote_copy(
                src_ref=cgt.at[pl.ds(pl.multiple_of(peer * piece, 8), piece), :],
                dst_ref=gathered.at[step],
                send_sem=cg_send.at[step], recv_sem=cg_recv.at[step],
                device_id=where, device_id_type=MESH,
            )

        for step in range(1, total):
            cg_copy(step).start()

    @pl.when(z < shards - 1)
    def _():
        def take(h, carry):
            edge_copy(h).wait_recv()
            return carry

        lax.fori_loop(0, heads, take, 0)

    for h in range(heads):
        for s in range(3):
            lanes = slice(h * width, (h + 1) * width)
            extra = tail[h, s * 8:s * 8 + 8, :] + edge_in[h, s * 8:s * 8 + 8, :]
            grads[s][count - 8:, lanes] = extra.astype(BF16)

    @pl.when(z < shards - 1)
    def _():
        halo_copy().wait_send()

        def sent(h, carry):
            state_copy(h).wait_send()
            return carry

        lax.fori_loop(0, heads, sent, 0)

    @pl.when(z > 0)
    def _():
        def sent(h, carry):
            adj_copy(h).wait_send()
            edge_copy(h).wait_send()
            return carry

        lax.fori_loop(0, heads, sent, 0)

    if scatter:
        sums = cgt[pl.ds(pl.multiple_of(mine * piece, 8), piece), :]
        for step in range(1, total):
            cg_copy(step).wait_recv()
            sums = sums + gathered[step]
        conv_out[...] = sums
        for step in range(1, total):
            cg_copy(step).wait_send()
    else:
        conv_out[...] = cg[...]


def flush(count, *refs):
    blocks, rest = refs[:count], refs[count:]
    if len(rest) == count + 1:
        outs, sems = rest[:count], rest[count]
        extra = ()
    else:
        conv, outs, conv_out, sems, turned = rest[0], rest[1:count + 1], *rest[count + 1:]
        extra = ((turned, conv_out),)
    copies = [
        pltpu.make_async_copy(block, out, sems.at[i])
        for i, (block, out) in enumerate((*zip(blocks, outs), *extra))
    ]
    for copy in copies[:count]:
        copy.start()
    if extra:
        turned[...] = conv[...].T[:turned.shape[0]]
        copies[count].start()
    for copy in copies:
        copy.wait()


def per_device(query_raw, key_raw, value_raw, conv_weight, beta_logit, cotangent):
    shards, parts = lax.axis_size("seq"), lax.axis_size("dp")
    heads = beta_logit.shape[1]
    count, channels = query_raw.shape[1:]
    width = channels // heads
    taps = conv_weight.shape[1]
    total = shards * parts
    scatter = total > 1 and width % (8 * total) == 0
    piece = width // total if scatter else 8
    slots = total if scatter else 2
    square = lambda dtype=F32, cols=width: pltpu.VMEM((heads, count, cols), dtype)
    dma = pltpu.SemaphoreType.DMA
    vmem = pl.BlockSpec(memory_space=pltpu.VMEM)
    conv_rows = piece if scatter else width
    levels = max(1, (count // TILE - 1).bit_length())
    outs = pl.pallas_call(
        functools.partial(kernel, shards, parts, scatter),
        out_shape=(
            jax.ShapeDtypeStruct((count, channels), F32),
            jax.ShapeDtypeStruct((count, channels), BF16),
            jax.ShapeDtypeStruct((count, channels), BF16),
            jax.ShapeDtypeStruct((count, channels), BF16),
            jax.ShapeDtypeStruct((heads, count), F32),
            jax.ShapeDtypeStruct((conv_rows, 128), F32),
        ),
        in_specs=[pl.BlockSpec(memory_space=pltpu.HBM)] * 6,
        out_specs=[vmem] * 6,
        scratch_shapes=[
            pltpu.VMEM((count, channels), BF16),
            pltpu.VMEM((count, channels), BF16),
            pltpu.VMEM((count, channels), BF16),
            pltpu.VMEM((3, taps, channels), F32),
            pltpu.VMEM((heads, count), F32),
            pltpu.VMEM((count, channels), BF16),
            pltpu.VMEM((16, channels), BF16),
            pltpu.VMEM((16, channels), BF16),
            pltpu.VMEM((3, 8, channels), F32),
            square(), square(), square(),
            pltpu.VMEM((3, heads, count, width), F32),
            *[square() for _ in range(3)],
            *[square(BF16, 2 * width) for _ in range(11)],
            square(),
            pltpu.VMEM((3 * heads, count + 16, width), F32),
            pltpu.VMEM((levels, count, count), BF16),
            square(), square(),
            square(BF16), square(BF16), square(BF16), square(BF16),
            pltpu.VMEM((heads, 24, width), F32),
            pltpu.VMEM((heads, 24, width), F32),
            pltpu.VMEM((heads, 24, width), F32),
            pltpu.VMEM((128, width), F32),
            pltpu.VMEM((width, 128), F32),
            pltpu.VMEM((slots, piece, 128), F32),
            dma, dma,
            dma((heads,)), dma((heads,)), dma((heads,)), dma((heads,)),
            dma((heads,)), dma((heads,)), dma((slots,)), dma((slots,)), dma((6,)),
            pltpu.SemaphoreType.REGULAR,
        ],
        compiler_params=pltpu.CompilerParams(
            collective_id=0, has_side_effects=True, vmem_limit_bytes=48 << 20
        ),
    )(
        *(
            pltpu.with_memory_space_constraint(x, pltpu.HBM)
            for x in (
                query_raw[0], key_raw[0], value_raw[0],
                conv_weight, beta_logit[0], cotangent[0],
            )
        )
    )
    used = 3 * taps * heads
    blocks, conv = outs[:5], outs[5]
    held, free = pl.BlockSpec(memory_space=pl.ANY), pl.BlockSpec(memory_space=pltpu.HBM)
    extra_shape = (jax.ShapeDtypeStruct((used, piece), F32),) if scatter else ()
    flushed = pl.pallas_call(
        functools.partial(flush, 5),
        out_shape=(*(jax.ShapeDtypeStruct(x.shape, x.dtype) for x in blocks), *extra_shape),
        in_specs=[held] * 5 + [vmem] * len(extra_shape),
        out_specs=[free] * (5 + len(extra_shape)),
        scratch_shapes=[
            dma((5 + len(extra_shape),)),
            *(pltpu.VMEM(x.shape, F32) for x in extra_shape),
        ],
        compiler_params=pltpu.CompilerParams(vmem_limit_bytes=2 << 20),
    )(*blocks, *((conv,) if scatter else ()))
    mixed, d_query, d_key, d_value, d_beta = flushed[:5]
    if scatter:
        conv_grad = flushed[5].reshape(3, taps, heads, piece)
    else:
        conv_grad = lax.psum_scatter(
            conv[:used].reshape(3, taps, heads, width),
            ("seq", "dp"), scatter_dimension=3, tiled=True,
        )
    return (mixed[None], d_query[None], d_key[None], d_value[None], d_beta[None], conv_grad)


def solution(mesh):
    rows = P(("group", "dp"), "seq", "head")
    in_specs = (
        rows, rows, rows,
        P(None, None, "head"),
        P(("group", "dp"), "head", "seq"),
        rows,
    )
    out_specs = (
        rows, rows, rows, rows,
        P(("group", "dp"), "head", "seq"),
        P("group", None, "head", ("seq", "dp")),
    )
    return jax.shard_map(
        per_device, mesh=mesh, in_specs=in_specs, out_specs=out_specs, check_vma=False
    )
```

```python
import functools
import itertools

import jax
import jax.numpy as jnp
from jax import lax
from jax.experimental import pallas as pl
from jax.experimental.pallas import tpu as pltpu
from jax.sharding import PartitionSpec as P

MESH = pl.DeviceIdType.MESH
F32 = jnp.float32
BF16 = jnp.bfloat16
GROUP = 4
PAIR = 2
TILE = 16
RAISE = 16384.0


def pair(x):
    high = x.astype(BF16)
    return high, (x - high.astype(F32)).astype(BF16)


def left(p):
    return jnp.concatenate(p, axis=1)


def rows_of(p):
    both = jnp.concatenate(p, axis=1)
    return jnp.concatenate([both, both], axis=0)


def turned(*ps):
    return jnp.concatenate(
        [jnp.concatenate([x for p in ps for x in (p[i], p[i])], axis=1) for i in (0, 1)],
        axis=0,
    )


def flipped(p):
    return p[0].T, p[1].T


def stack(*xs):
    return jnp.concatenate(xs, axis=0)


def dot(a, b, flip=False):
    return lax.dot_general(
        a, b, (((1,), (1 if flip else 0,)), ((), ())), preferred_element_type=F32
    )


def fold(x):
    n = x.shape[1] // 2
    return x[:, :n] + x[:, n:]


def halves(ref, h):
    both = ref[h]
    n = both.shape[1] // 2
    return both[:, :n], both[:, n:]


def encode(x):
    x = x * RAISE
    square = x * x
    return (x * jnp.abs(x) * square).astype(BF16)


def decode(code):
    code = code.astype(F32)
    size = jnp.abs(code)
    root = jnp.where(size > 0.0, lax.rsqrt(lax.rsqrt(size)), 0.0) * (1.0 / RAISE)
    return jnp.where(code < 0.0, -root, root)


def kernel(
    shards, parts, scatter,
    q_hbm, k_hbm, v_hbm, conv_hbm, beta_hbm, cot_hbm,
    mixed_ref, dq_ref, dk_ref, dv_ref, dbeta_ref, conv_out,
    q_raw, k_raw, v_raw, conv_ref, beta_ref, cot_ref,
    halo_out, halo_in, before, q_s, k_s, v_s, g_s, bcol_s, pu_s, pg_s,
    kp_s, qp_s, tp_s, wp_s, up_s, rp_s, np_s, ntp_s, sp_s, cp_s, yp_s, dk_s, shift_s, masks,
    loc_state, loc_adj, out_state, out_adj, in_state, in_adj,
    edge_out, edge_in, tail, cg, cgt, gathered,
    halo_send, halo_recv, state_send, state_recv, adj_send, adj_recv,
    edge_send, edge_recv, cg_send, cg_recv, load_sem, beside,
):
    z = lax.axis_index("seq")
    heads = beta_ref.shape[0]
    count, width = q_raw.shape[0], q_raw.shape[1] // heads
    first, last = z == 0, z == shards - 1
    raws = (q_raw, k_raw, v_raw)
    acts = (q_s, k_s, v_s)
    sources = (q_hbm, k_hbm, v_hbm, conv_hbm, beta_hbm, cot_hbm)
    loads = [
        pltpu.make_async_copy(source, kept, load_sem.at[i])
        for i, (source, kept) in enumerate(
            zip(sources, (q_raw, k_raw, v_raw, conv_ref, beta_ref, cot_ref))
        )
    ]
    for load in loads:
        load.start()
    grads = (dq_ref, dk_ref, dv_ref)

    barrier = pltpu.get_barrier_semaphore()
    if scatter:
        total = shards * parts
        column = lax.axis_index("dp")
        mine = z * parts + column

        def peer_of(step):
            peer = lax.rem(mine + step, total)
            return peer, {"seq": peer // parts, "dp": lax.rem(peer, parts)}

        def beside_of(step):
            return {"dp": lax.rem(column + step, parts)}

        for step in range(1, parts):
            pl.semaphore_signal(
                barrier, inc=1, device_id=beside_of(step), device_id_type=MESH
            )

    @pl.when(z > 0)
    def _():
        pl.semaphore_signal(barrier, inc=1, device_id={"seq": z - 1}, device_id_type=MESH)

    @pl.when(z < shards - 1)
    def _():
        pl.semaphore_signal(barrier, inc=1, device_id={"seq": z + 1}, device_id_type=MESH)

    met = parts - 1 if scatter else 0

    def all_of(source, target, send, recv, to):
        return pltpu.make_async_remote_copy(
            src_ref=source, dst_ref=target, send_sem=send, recv_sem=recv,
            device_id={"seq": to}, device_id_type=MESH,
        )

    def halo_copy():
        return pltpu.make_async_remote_copy(
            src_ref=halo_out, dst_ref=halo_in,
            send_sem=halo_send, recv_sem=halo_recv,
            device_id={"seq": z + 1}, device_id_type=MESH,
        )

    def state_copy(h):
        return pltpu.make_async_remote_copy(
            src_ref=out_state.at[h], dst_ref=in_state.at[h],
            send_sem=state_send, recv_sem=state_recv.at[h],
            device_id={"seq": z + 1}, device_id_type=MESH,
        )

    def adj_copy(h):
        return pltpu.make_async_remote_copy(
            src_ref=out_adj.at[h], dst_ref=in_adj.at[h],
            send_sem=adj_send, recv_sem=adj_recv.at[h],
            device_id={"seq": z - 1}, device_id_type=MESH,
        )

    def edge_copy(h):
        return pltpu.make_async_remote_copy(
            src_ref=edge_out.at[h], dst_ref=edge_in.at[h],
            send_sem=edge_send, recv_sem=edge_recv,
            device_id={"seq": z - 1}, device_id_type=MESH,
        )

    rows = lax.broadcasted_iota(jnp.int32, (count, count), 0)
    cols = lax.broadcasted_iota(jnp.int32, (count, count), 1)
    apart = rows ^ cols
    strict = rows > cols
    lower = rows >= cols
    eye = rows == cols
    near = apart < TILE
    sizes = []
    while (TILE << len(sizes)) < count:
        sizes.append(TILE << len(sizes))
    for i, size in enumerate(sizes):
        band = (apart >= size) & (apart < 2 * size)
        masks[i] = jnp.where(band, 1.0, 0.0).astype(BF16)
    cg[...] = jnp.zeros_like(cg)

    @pl.when(first)
    def _():
        in_state[...] = jnp.zeros_like(in_state)
        before[...] = jnp.zeros_like(before)

    @pl.when(last)
    def _():
        in_adj[...] = jnp.zeros_like(in_adj)
        edge_in[...] = jnp.zeros_like(edge_in)

    def lanes_of(h):
        return pl.ds(pl.multiple_of(h * width, width), width)

    for slot in range(shift_s.shape[0]):
        shift_s[slot, :8] = jnp.zeros((8, width), F32)
        shift_s[slot, 8 + count:] = jnp.zeros((8, width), F32)

    for load in loads:
        load.wait()

    @pl.when(z < shards - 1)
    def _():
        ends = [raw[count - 16:, :].astype(F32)[12:] for raw in raws]
        halo_out[...] = stack(*ends, jnp.zeros_like(ends[0])).astype(BF16)

    def activate(s, h, piece, n):
        lanes = lanes_of(h)
        taps = [conv_ref[s, j:j + 1, lanes] for j in range(4)]
        for at in range(0, n, 8):
            pre = taps[0] * piece(at + 5)
            for j in range(1, 4):
                pre = pre + taps[j] * piece(at + j + 5)
            gate = 1.0 / (1.0 + jnp.exp(-pre))
            act = pre * gate
            slope = gate * (1.0 + pre * (1.0 - gate))
            if s < 2:
                scale = lax.rsqrt(jnp.sum(act * act, axis=1, keepdims=True) + 1e-06)
                act = act * scale
                slope = slope * scale
            acts[s][h, at:at + 8] = act
            g_s[s, h, at:at + 8] = slope

    def convolve(h, carry):
        for s in range(3):
            slot = h * 3 + s
            shift_s[slot, 8:8 + count] = raws[s][:, lanes_of(h)].astype(F32)
            activate(s, h, lambda at, slot=slot: shift_s[slot, at:at + 8], count)
        row = 1.0 / (1.0 + jnp.exp(-beta_ref[pl.ds(h, 1), :]))
        column = jnp.sum(jnp.where(eye, row, 0.0), axis=1, keepdims=True)
        bcol_s[h] = jnp.broadcast_to(column, (count, width))
        return carry

    ahead = jnp.where(first, heads * 3 // 4, 0)
    lax.fori_loop(0, ahead, convolve, 0)

    @pl.when((z > 0) & (z < shards - 1))
    def _():
        pl.semaphore_wait(barrier, met + 2)

    @pl.when(first | last)
    def _():
        pl.semaphore_wait(barrier, met + 1)

    @pl.when(z < shards - 1)
    def _():
        halo_copy().start()

    lax.fori_loop(ahead, heads, convolve, 0)

    @pl.when(z > 0)
    def _():
        halo_copy().wait_recv()
        ends = halo_in[...].astype(F32)
        for s in range(3):
            three = ends[4 * s + 1:4 * s + 4]
            before[s] = stack(jnp.zeros((5, three.shape[1]), F32), three)
            for h in range(heads):
                lanes = slice(h * width, (h + 1) * width)
                ext = stack(before[s, :, lanes], raws[s][:16, lanes].astype(F32)[:8])
                activate(s, h, lambda at, ext=ext: ext[at:at + 8], 8)

    def advance(both, value):
        return value - fold(dot(both, rows_of(pair(value))))

    quads = heads // GROUP

    def pass_state(h):
        state_copy(h).wait_recv()

        @pl.when(z < shards - 1)
        def _():
            out_state[h] = encode(loc_state[h] + advance(np_s[h], decode(in_state[h])))
            state_copy(h).start()

    def pass_adjoint(h):
        adj_copy(h).wait_recv()

        @pl.when(z > 0)
        def _():
            out_adj[h] = encode(loc_adj[h] + advance(ntp_s[h], decode(in_adj[h])))
            adj_copy(h).start()

    def forward(qs, qa, least):
        def one(i, carry):
            @pl.when((qs >= 0) & (qs < quads) & (z >= least))
            def _():
                pass_state(qs * GROUP + i)

            @pl.when((qa >= 0) & (qa < quads) & (z < shards - 1))
            def _():
                pass_adjoint(qa * GROUP + i)

            return carry

        lax.fori_loop(0, GROUP, one, 0)

    def prepare(step, carry):
        ids = [step * GROUP + i for i in range(GROUP)]
        each = range(GROUP)
        qs = [q_s[h] for h in ids]
        k2 = [pair(k_s[h]) for h in ids]
        q2 = [pair(x) for x in qs]
        both = [
            fold(dot(stack(left(k), left(q)), turned(k), True)) for k, q in zip(k2, q2)
        ]
        gram = [x[:count] for x in both]
        p2 = [pair(jnp.where(lower, x[count:], 0.0)) for x in both]
        low = [jnp.where(strict, bcol_s[h] * g, 0.0) for h, g in zip(ids, gram)]
        l2 = [pair(x) for x in low]
        small = [
            jnp.sum(jnp.where(near, x, 0.0).reshape(count // TILE, TILE, count), axis=0)
            for x in low
        ]
        lane = lax.broadcasted_iota(jnp.int32, (8, count), 1)
        base = lane - lax.rem(lane, TILE)
        row8 = lax.broadcasted_iota(jnp.int32, (8, count), 0)
        parts8 = TILE // 8
        x8 = [
            [jnp.where(lane - base == row8 + 8 * p, 1.0, 0.0) for p in range(parts8)]
            for _ in each
        ]
        for j in range(TILE - 1):
            for x, m in zip(x8, small):
                pivot = x[j // 8][j % 8:j % 8 + 1]
                for p in range(j // 8, parts8):
                    column = jnp.take_along_axis(
                        m[8 * p:8 * p + 8], base + j, axis=1, mode="promise_in_bounds"
                    )
                    x[p] = x[p] - column * pivot
        x8 = [stack(*x) for x in x8]
        inv = [jnp.where(near, stack(*[x] * (count // TILE)), 0.0) for x in x8]
        for level in range(len(sizes)):
            mask = masks[level]
            i2 = [pair(x) for x in inv]
            part = [
                fold(dot(left(m), rows_of((a[0] * mask, a[1] * mask))))
                for m, a in zip(i2, l2)
            ]
            inv = [
                m - fold(dot(left(pair(x)), rows_of(n))) for m, x, n in zip(inv, part, i2)
            ]
        t2 = [pair(x) for x in inv]
        scaled = [
            left(pair(m * (1.0 / (1.0 + jnp.exp(-beta_ref[pl.ds(h, 1), :])))))
            for h, m in zip(ids, inv)
        ]
        w2 = [pair(fold(dot(t, rows_of(k)))) for t, k in zip(scaled, k2)]
        u2 = [pair(fold(dot(t, rows_of(pair(v_s[h]))))) for h, t in zip(ids, scaled)]
        onto = [stack(left(flipped(k)), left(p)) for k, p in zip(k2, p2)]
        on_w = [fold(dot(a, rows_of(w))) for a, w in zip(onto, w2)]
        on_u = [fold(dot(a, rows_of(u))) for a, u in zip(onto, u2)]
        r2 = [pair(q - x[count:]) for q, x in zip(qs, on_w)]
        n2 = [pair(x[:width]) for x in on_w]
        cots = [cot_ref[:, lanes_of(h)] for h in ids]
        back = [
            dot(stack(left(flipped(r)), left(flipped(p))), stack(c, c))
            for r, p, c in zip(r2, p2, cots)
        ]

        @pl.when(first)
        def _():
            for i, h in enumerate(ids):
                out_state[h] = encode(on_u[i][:width])
                state_copy(h).start()

        @pl.when(last)
        def _():
            for i, h in enumerate(ids):
                out_adj[h] = encode(back[i][:width])
                adj_copy(h).start()

        for i, h in enumerate(ids):
            loc_state[h] = on_u[i][:width]
            loc_adj[h] = back[i][:width]
            pu_s[h] = on_u[i][width:]
            pg_s[h] = back[i][width:]
            kp_s[h] = left(k2[i])
            qp_s[h] = left(q2[i])
            tp_s[h] = left(flipped(t2[i]))
            wp_s[h] = left(w2[i])
            up_s[h] = left(u2[i])
            rp_s[h] = left(r2[i])
            np_s[h] = left(n2[i])
            ntp_s[h] = left(flipped(n2[i]))

        @pl.when(z == 1)
        def _():
            forward(step, -1, 1)

        return carry

    lax.fori_loop(0, heads // GROUP, prepare, 0)

    def conv_back(s, h, grad):
        lanes, slot = lanes_of(h), h * 3 + s
        if s < 2:
            unit = acts[s][h]
            grad = grad - unit * jnp.sum(grad * unit, axis=1, keepdims=True)
        shift_s[slot, 8:8 + count] = grad * g_s[s, h]
        yield
        taps = [conv_ref[s, j:j + 1, lanes] for j in range(4)]
        sums = [None] * 4
        for at in range(0, count + 8, 8):
            if at == 0:
                series = before[s, :, lanes]
            elif at % 16 == 8:
                both = raws[s][at - 8:at + 8, lanes].astype(F32)
                series = both[:8]
            else:
                series = both[8:]
            full = None
            for j in range(4):
                moved = shift_s[slot, at + 3 - j:at + 11 - j]
                term, product = taps[j] * moved, series * moved
                full = term if full is None else full + term
                sums[j] = product if sums[j] is None else sums[j] + product
            if at == 0:
                edge_out[h, s * 8:s * 8 + 8, :] = full
            elif at % 16 == 8:
                held = full
            else:
                grads[s][at - 16:at, lanes] = stack(held, full).astype(BF16)
        tail[h, s * 8:s * 8 + 8, :] = full
        for j in range(4):
            cg[pl.ds((s * 4 + j) * heads + h, 1), :] = jnp.sum(sums[j], axis=0, keepdims=True)

    def state_part(h, keep):
        lanes = lanes_of(h)
        cot = cot_ref[:, lanes]
        state2 = pair(decode(in_state[h]))
        k2, q2, u2 = (halves(x, h) for x in (kp_s, qp_s, up_s))
        reads = fold(dot(stack(wp_s[h], rp_s[h]), rows_of(state2)))
        d_query = fold(dot(cot, stack(*state2), True))
        yield
        mixed_ref[:, lanes] = reads[count:] + pu_s[h]
        corr2 = pair((u2[0].astype(F32) - reads[:count]) + u2[1].astype(F32))
        yield
        ds2 = pair(jnp.where(lower, fold(dot(cot, stack(*corr2), True)), 0.0))
        yield
        d_query = d_query + fold(dot(left(ds2), rows_of(k2)))
        d_key = fold(dot(left(flipped(ds2)), rows_of(q2)))
        keep.update(state2=state2, corr2=corr2, d_key=d_key)
        yield
        yield from conv_back(0, h, d_query)

    def adjoint_part(h, keep):
        adj2 = pair(decode(in_adj[h]))
        dc2 = pair(pg_s[h] + fold(dot(kp_s[h], rows_of(adj2))))
        yield
        y_v = fold(dot(tp_s[h], rows_of(dc2)))
        keep.update(adj2=adj2, yv2=pair(y_v))
        yield
        yield from conv_back(2, h, bcol_s[h] * y_v)

    def last_part(h, keep):
        corr2, yv2 = keep["corr2"], keep["yv2"]
        ys = left(yv2)
        d_gram = jnp.where(strict, -bcol_s[h] * fold(dot(ys, turned(corr2), True)), 0.0)
        y_k = -fold(dot(ys, turned(keep["state2"]), True))
        yield
        d_key = (
            keep["d_key"] + bcol_s[h] * y_k
            + fold(dot(left(corr2), turned(keep["adj2"]), True))
            + fold(dot(left(pair(d_gram + d_gram.T)), rows_of(halves(kp_s, h))))
        )
        yield
        inner = sum(x.astype(F32) for x in yv2) * sum(x.astype(F32) for x in corr2)
        column = jnp.sum(inner, axis=1, keepdims=True)
        row = jnp.sum(jnp.where(eye, column, 0.0), axis=0, keepdims=True)
        dbeta_ref[pl.ds(h, 1), :] = row / (1.0 + jnp.exp(beta_ref[pl.ds(h, 1), :]))
        yield from conv_back(1, h, d_key)

    def together(gens):
        for _ in itertools.zip_longest(*gens):
            pass

    def chained(*gens):
        for gen in gens:
            yield from gen

    early = z < shards // 2

    def group_of(q):
        return [q * GROUP + i for i in range(GROUP)]

    def send_edges(ids):
        @pl.when(z > 0)
        def _():
            for h in ids:
                edge_copy(h).start()

    def chain(step, carry):
        ids = group_of(step)
        keeps = [{} for _ in ids]

        @pl.when(early)
        def _():
            forward(step, jnp.where(first, -1, step - 1), 2)
            together([state_part(h, keep) for h, keep in zip(ids, keeps)])
            for h, keep in zip(ids, keeps):
                sp_s[h] = left(keep["state2"])
                cp_s[h] = left(keep["corr2"])
                dk_s[h] = keep["d_key"]

        @pl.when(jnp.logical_not(early))
        def _():
            forward(-1, step, 2)
            forward(jnp.where(last, -1, step), -1, 2)
            together([adjoint_part(h, keep) for h, keep in zip(ids, keeps)])
            for h, keep in zip(ids, keeps):
                sp_s[h] = left(keep["adj2"])
                yp_s[h] = left(keep["yv2"])

        if scatter:
            @pl.when(step == 1)
            def _():
                for other in range(1, parts):
                    pl.semaphore_signal(
                        beside, inc=1, device_id=beside_of(other), device_id_type=MESH
                    )

        return carry

    lax.fori_loop(0, quads, chain, 0)

    @pl.when(early & (z > 0))
    def _():
        forward(-1, quads - 1, 2)

    def complete(step, carry):
        ids = [step * PAIR + i for i in range(PAIR)]

        @pl.when(first & (z < shards - 1))
        def _():
            for h in ids:
                adj_copy(h).wait_recv()

        @pl.when(last & (z > 1))
        def _():
            for h in ids:
                state_copy(h).wait_recv()

        @pl.when(early)
        def _():
            keeps = [
                {"state2": halves(sp_s, h), "corr2": halves(cp_s, h), "d_key": dk_s[h]}
                for h in ids
            ]
            together([
                chained(adjoint_part(h, keep), last_part(h, keep))
                for h, keep in zip(ids, keeps)
            ])

        @pl.when(jnp.logical_not(early))
        def _():
            keeps = [{"adj2": halves(sp_s, h), "yv2": halves(yp_s, h)} for h in ids]
            together([
                chained(state_part(h, keep), last_part(h, keep))
                for h, keep in zip(ids, keeps)
            ])

        send_edges(ids)
        return carry

    lax.fori_loop(0, heads // PAIR, complete, 0)

    if scatter:
        if parts > 1:
            pl.semaphore_wait(beside, parts - 1)
        piece = cgt.shape[0] // total
        cgt[...] = cg[...].T

        def cg_copy(step):
            peer, where = peer_of(step)
            return pltpu.make_async_remote_copy(
                src_ref=cgt.at[pl.ds(pl.multiple_of(peer * piece, 8), piece), :],
                dst_ref=gathered.at[step],
                send_sem=cg_send, recv_sem=cg_recv,
                device_id=where, device_id_type=MESH,
            )

        for step in range(1, total):
            cg_copy(step).start()

    @pl.when(z < shards - 1)
    def _():
        all_of(edge_out, edge_in, edge_send, edge_recv, z + 1).wait_recv()

    for h in range(heads):
        for s in range(3):
            lanes = slice(h * width, (h + 1) * width)
            extra = tail[h, s * 8:s * 8 + 8, :] + edge_in[h, s * 8:s * 8 + 8, :]
            grads[s][count - 8:, lanes] = extra.astype(BF16)

    @pl.when(z < shards - 1)
    def _():
        halo_copy().wait_send()

        all_of(out_state, in_state, state_send, state_recv.at[0], z + 1).wait_send()

    @pl.when(z > 0)
    def _():
        all_of(out_adj, in_adj, adj_send, adj_recv.at[0], z - 1).wait_send()
        all_of(edge_out, edge_in, edge_send, edge_recv, z - 1).wait_send()

    if scatter:
        sums = cgt[pl.ds(pl.multiple_of(mine * piece, 8), piece), :]
        others = gathered.at[pl.ds(1, total - 1)]
        everyone = all_of(others, others, cg_send, cg_recv, lax.rem(z + 1, shards))
        everyone.wait_recv()
        for step in range(1, total):
            sums = sums + gathered[step]
        conv_out[...] = sums
        everyone.wait_send()
    else:
        conv_out[...] = cg[...]


def flush(count, *refs):
    blocks, rest = refs[:count], refs[count:]
    if len(rest) == count + 1:
        outs, sems = rest[:count], rest[count]
        extra = ()
    else:
        conv, outs, conv_out, sems, turned = rest[0], rest[1:count + 1], *rest[count + 1:]
        extra = ((turned, conv_out),)
    copies = [
        pltpu.make_async_copy(block, out, sems.at[i])
        for i, (block, out) in enumerate((*zip(blocks, outs), *extra))
    ]
    for copy in copies[:count]:
        copy.start()
    if extra:
        turned[...] = conv[...].T[:turned.shape[0]]
        copies[count].start()
    for copy in copies:
        copy.wait()


def per_device(query_raw, key_raw, value_raw, conv_weight, beta_logit, cotangent):
    shards, parts = lax.axis_size("seq"), lax.axis_size("dp")
    heads = beta_logit.shape[1]
    count, channels = query_raw.shape[1:]
    width = channels // heads
    taps = conv_weight.shape[1]
    total = shards * parts
    scatter = total > 1 and width % (8 * total) == 0
    piece = width // total if scatter else 8
    slots = total if scatter else 2
    square = lambda dtype=F32, cols=width: pltpu.VMEM((heads, count, cols), dtype)
    dma = pltpu.SemaphoreType.DMA
    vmem = pl.BlockSpec(memory_space=pltpu.VMEM)
    conv_rows = piece if scatter else width
    levels = max(1, (count // TILE - 1).bit_length())
    outs = pl.pallas_call(
        functools.partial(kernel, shards, parts, scatter),
        out_shape=(
            jax.ShapeDtypeStruct((count, channels), F32),
            jax.ShapeDtypeStruct((count, channels), BF16),
            jax.ShapeDtypeStruct((count, channels), BF16),
            jax.ShapeDtypeStruct((count, channels), BF16),
            jax.ShapeDtypeStruct((heads, count), F32),
            jax.ShapeDtypeStruct((conv_rows, 128), F32),
        ),
        in_specs=[pl.BlockSpec(memory_space=pltpu.HBM)] * 6,
        out_specs=[vmem] * 6,
        scratch_shapes=[
            pltpu.VMEM((count, channels), BF16),
            pltpu.VMEM((count, channels), BF16),
            pltpu.VMEM((count, channels), BF16),
            pltpu.VMEM((3, taps, channels), F32),
            pltpu.VMEM((heads, count), F32),
            pltpu.VMEM((count, channels), BF16),
            pltpu.VMEM((16, channels), BF16),
            pltpu.VMEM((16, channels), BF16),
            pltpu.VMEM((3, 8, channels), F32),
            square(), square(), square(),
            pltpu.VMEM((3, heads, count, width), F32),
            *[square() for _ in range(3)],
            *[square(BF16, 2 * width) for _ in range(11)],
            square(),
            pltpu.VMEM((3 * heads, count + 16, width), F32),
            pltpu.VMEM((levels, count, count), BF16),
            square(), square(),
            square(BF16), square(BF16), square(BF16), square(BF16),
            pltpu.VMEM((heads, 24, width), F32),
            pltpu.VMEM((heads, 24, width), F32),
            pltpu.VMEM((heads, 24, width), F32),
            pltpu.VMEM((128, width), F32),
            pltpu.VMEM((width, 128), F32),
            pltpu.VMEM((slots, piece, 128), F32),
            dma, dma,
            dma, dma((heads,)), dma, dma((heads,)),
            dma, dma, dma, dma, dma((6,)),
            pltpu.SemaphoreType.REGULAR,
        ],
        compiler_params=pltpu.CompilerParams(
            collective_id=0, has_side_effects=True, vmem_limit_bytes=48 << 20
        ),
    )(
        *(
            pltpu.with_memory_space_constraint(x, pltpu.HBM)
            for x in (
                query_raw[0], key_raw[0], value_raw[0],
                conv_weight, beta_logit[0], cotangent[0],
            )
        )
    )
    used = 3 * taps * heads
    blocks, conv = outs[:5], outs[5]
    held, free = pl.BlockSpec(memory_space=pl.ANY), pl.BlockSpec(memory_space=pltpu.HBM)
    extra_shape = (jax.ShapeDtypeStruct((used, piece), F32),) if scatter else ()
    flushed = pl.pallas_call(
        functools.partial(flush, 5),
        out_shape=(*(jax.ShapeDtypeStruct(x.shape, x.dtype) for x in blocks), *extra_shape),
        in_specs=[held] * 5 + [vmem] * len(extra_shape),
        out_specs=[free] * (5 + len(extra_shape)),
        scratch_shapes=[
            dma((5 + len(extra_shape),)),
            *(pltpu.VMEM(x.shape, F32) for x in extra_shape),
        ],
        compiler_params=pltpu.CompilerParams(vmem_limit_bytes=2 << 20),
    )(*blocks, *((conv,) if scatter else ()))
    mixed, d_query, d_key, d_value, d_beta = flushed[:5]
    if scatter:
        conv_grad = flushed[5].reshape(3, taps, heads, piece)
    else:
        conv_grad = lax.psum_scatter(
            conv[:used].reshape(3, taps, heads, width),
            ("seq", "dp"), scatter_dimension=3, tiled=True,
        )
    return (mixed[None], d_query[None], d_key[None], d_value[None], d_beta[None], conv_grad)


def solution(mesh):
    rows = P(("group", "dp"), "seq", "head")
    in_specs = (
        rows, rows, rows,
        P(None, None, "head"),
        P(("group", "dp"), "head", "seq"),
        rows,
    )
    out_specs = (
        rows, rows, rows, rows,
        P(("group", "dp"), "head", "seq"),
        P("group", None, "head", ("seq", "dp")),
    )
    return jax.shard_map(
        per_device, mesh=mesh, in_specs=in_specs, out_specs=out_specs, check_vma=False
    )
```

```python
import functools
import itertools

import jax
import jax.numpy as jnp
from jax import lax
from jax.experimental import pallas as pl
from jax.experimental.pallas import tpu as pltpu
from jax.sharding import PartitionSpec as P

MESH = pl.DeviceIdType.MESH
F32 = jnp.float32
BF16 = jnp.bfloat16
GROUP = 4
PAIR = 2
TILE = 16
RAISE = 16384.0


def pair(x):
    high = x.astype(BF16)
    return high, (x - high.astype(F32)).astype(BF16)


def left(p):
    return jnp.concatenate(p, axis=1)


def rows_of(p):
    both = jnp.concatenate(p, axis=1)
    return jnp.concatenate([both, both], axis=0)


def turned(*ps):
    return jnp.concatenate(
        [jnp.concatenate([x for p in ps for x in (p[i], p[i])], axis=1) for i in (0, 1)],
        axis=0,
    )


def flipped(p):
    return p[0].T, p[1].T


def stack(*xs):
    return jnp.concatenate(xs, axis=0)


def dot(a, b, flip=False):
    return lax.dot_general(
        a, b, (((1,), (1 if flip else 0,)), ((), ())), preferred_element_type=F32
    )


def fold(x):
    n = x.shape[1] // 2
    return x[:, :n] + x[:, n:]


def halves(ref, h):
    both = ref[h]
    n = both.shape[1] // 2
    return both[:, :n], both[:, n:]


def encode(x):
    x = x * RAISE
    square = x * x
    return (x * jnp.abs(x) * square).astype(BF16)


def decode(code):
    code = code.astype(F32)
    size = jnp.abs(code)
    root = jnp.where(size > 0.0, lax.rsqrt(lax.rsqrt(size)), 0.0) * (1.0 / RAISE)
    return jnp.where(code < 0.0, -root, root)


def kernel(
    shards, parts, scatter,
    q_hbm, k_hbm, v_hbm, conv_hbm, beta_hbm, cot_hbm,
    mixed_ref, dq_ref, dk_ref, dv_ref, dbeta_ref, conv_out,
    q_raw, k_raw, v_raw, conv_ref, beta_ref, cot_ref,
    halo_out, halo_in, before, q_s, k_s, v_s, g_s, bcol_s, pu_s, pg_s,
    kp_s, qp_s, tp_s, wp_s, up_s, rp_s, np_s, ntp_s, sp_s, cp_s, yp_s, dk_s, shift_s, masks,
    loc_state, loc_adj, out_state, out_adj, in_state, in_adj,
    edge_out, edge_in, tail, cg, cgt, gathered,
    halo_send, halo_recv, state_send, state_recv, adj_send, adj_recv,
    edge_send, edge_recv, cg_send, cg_recv, load_sem, beside,
):
    z = lax.axis_index("seq")
    heads = beta_ref.shape[0]
    count, width = q_raw.shape[0], q_raw.shape[1] // heads
    first, last = z == 0, z == shards - 1
    raws = (q_raw, k_raw, v_raw)
    acts = (q_s, k_s, v_s)
    sources = (q_hbm, k_hbm, v_hbm, conv_hbm, beta_hbm, cot_hbm)
    loads = [
        pltpu.make_async_copy(source, kept, load_sem.at[i])
        for i, (source, kept) in enumerate(
            zip(sources, (q_raw, k_raw, v_raw, conv_ref, beta_ref, cot_ref))
        )
    ]
    for load in loads:
        load.start()
    grads = (dq_ref, dk_ref, dv_ref)

    barrier = pltpu.get_barrier_semaphore()
    if scatter:
        total = shards * parts
        column = lax.axis_index("dp")
        mine = z * parts + column

        def peer_of(step):
            peer = lax.rem(mine + step, total)
            return peer, {"seq": peer // parts, "dp": lax.rem(peer, parts)}

        def beside_of(step):
            return {"dp": lax.rem(column + step, parts)}

        for step in range(1, parts):
            pl.semaphore_signal(
                barrier, inc=1, device_id=beside_of(step), device_id_type=MESH
            )

    @pl.when(z > 0)
    def _():
        pl.semaphore_signal(barrier, inc=1, device_id={"seq": z - 1}, device_id_type=MESH)

    @pl.when(z < shards - 1)
    def _():
        pl.semaphore_signal(barrier, inc=1, device_id={"seq": z + 1}, device_id_type=MESH)

    met = parts - 1 if scatter else 0

    def all_of(source, target, send, recv, to):
        return pltpu.make_async_remote_copy(
            src_ref=source, dst_ref=target, send_sem=send, recv_sem=recv,
            device_id={"seq": to}, device_id_type=MESH,
        )

    def halo_copy():
        return pltpu.make_async_remote_copy(
            src_ref=halo_out, dst_ref=halo_in,
            send_sem=halo_send, recv_sem=halo_recv,
            device_id={"seq": z + 1}, device_id_type=MESH,
        )

    def state_copy(h):
        return pltpu.make_async_remote_copy(
            src_ref=out_state.at[h], dst_ref=in_state.at[h],
            send_sem=state_send, recv_sem=state_recv.at[h],
            device_id={"seq": z + 1}, device_id_type=MESH,
        )

    def adj_copy(h):
        return pltpu.make_async_remote_copy(
            src_ref=out_adj.at[h], dst_ref=in_adj.at[h],
            send_sem=adj_send, recv_sem=adj_recv.at[h],
            device_id={"seq": z - 1}, device_id_type=MESH,
        )

    def edge_copy(h):
        return pltpu.make_async_remote_copy(
            src_ref=edge_out.at[h], dst_ref=edge_in.at[h],
            send_sem=edge_send, recv_sem=edge_recv,
            device_id={"seq": z - 1}, device_id_type=MESH,
        )

    rows = lax.broadcasted_iota(jnp.int32, (count, count), 0)
    cols = lax.broadcasted_iota(jnp.int32, (count, count), 1)
    apart = rows ^ cols
    strict = rows > cols
    lower = rows >= cols
    eye = rows == cols
    near = apart < TILE
    sizes = []
    while (TILE << len(sizes)) < count:
        sizes.append(TILE << len(sizes))
    for i, size in enumerate(sizes):
        band = (apart >= size) & (apart < 2 * size)
        masks[i] = jnp.where(band, 1.0, 0.0).astype(BF16)
    cg[...] = jnp.zeros_like(cg)

    @pl.when(first)
    def _():
        in_state[...] = jnp.zeros_like(in_state)
        before[...] = jnp.zeros_like(before)

    @pl.when(last)
    def _():
        in_adj[...] = jnp.zeros_like(in_adj)
        edge_in[...] = jnp.zeros_like(edge_in)

    def lanes_of(h):
        return pl.ds(pl.multiple_of(h * width, width), width)

    for slot in range(shift_s.shape[0]):
        shift_s[slot, :8] = jnp.zeros((8, width), F32)
        shift_s[slot, 8 + count:] = jnp.zeros((8, width), F32)

    for load in loads:
        load.wait()

    @pl.when(z < shards - 1)
    def _():
        ends = [raw[count - 16:, :].astype(F32)[12:] for raw in raws]
        halo_out[...] = stack(*ends, jnp.zeros_like(ends[0])).astype(BF16)

    def activate(s, h, piece, n):
        lanes = lanes_of(h)
        taps = [conv_ref[s, j:j + 1, lanes] for j in range(4)]
        for at in range(0, n, 8):
            pre = taps[0] * piece(at + 5)
            for j in range(1, 4):
                pre = pre + taps[j] * piece(at + j + 5)
            gate = 1.0 / (1.0 + jnp.exp(-pre))
            act = pre * gate
            slope = gate * (1.0 + pre * (1.0 - gate))
            if s < 2:
                scale = lax.rsqrt(jnp.sum(act * act, axis=1, keepdims=True) + 1e-06)
                act = act * scale
                slope = slope * scale
            acts[s][h, at:at + 8] = act
            g_s[s, h, at:at + 8] = slope

    def convolve(h, carry):
        for s in range(3):
            slot = h * 3 + s
            shift_s[slot, 8:8 + count] = raws[s][:, lanes_of(h)].astype(F32)
            activate(s, h, lambda at, slot=slot: shift_s[slot, at:at + 8], count)
        row = 1.0 / (1.0 + jnp.exp(-beta_ref[pl.ds(h, 1), :]))
        column = jnp.sum(jnp.where(eye, row, 0.0), axis=1, keepdims=True)
        bcol_s[h] = jnp.broadcast_to(column, (count, width))
        return carry

    ahead = jnp.where(first, heads * 3 // 4, 0)
    lax.fori_loop(0, ahead, convolve, 0)

    @pl.when((z > 0) & (z < shards - 1))
    def _():
        pl.semaphore_wait(barrier, met + 2)

    @pl.when(first | last)
    def _():
        pl.semaphore_wait(barrier, met + 1)

    @pl.when(z < shards - 1)
    def _():
        halo_copy().start()

    lax.fori_loop(ahead, heads, convolve, 0)

    @pl.when(z > 0)
    def _():
        halo_copy().wait_recv()
        ends = halo_in[...].astype(F32)
        for s in range(3):
            three = ends[4 * s + 1:4 * s + 4]
            before[s] = stack(jnp.zeros((5, three.shape[1]), F32), three)
            for h in range(heads):
                lanes = slice(h * width, (h + 1) * width)
                ext = stack(before[s, :, lanes], raws[s][:16, lanes].astype(F32)[:8])
                activate(s, h, lambda at, ext=ext: ext[at:at + 8], 8)

    def advance(both, value):
        return value - fold(dot(both, rows_of(pair(value))))

    quads = heads // GROUP

    def pass_state(h):
        state_copy(h).wait_recv()

        @pl.when(z < shards - 1)
        def _():
            out_state[h] = encode(loc_state[h] + advance(np_s[h], decode(in_state[h])))
            state_copy(h).start()

    def pass_adjoint(h):
        adj_copy(h).wait_recv()

        @pl.when(z > 0)
        def _():
            out_adj[h] = encode(loc_adj[h] + advance(ntp_s[h], decode(in_adj[h])))
            adj_copy(h).start()

    def forward(qs, qa, least):
        def one(i, carry):
            @pl.when((qs >= 0) & (qs < quads) & (z >= least))
            def _():
                pass_state(qs * GROUP + i)

            @pl.when((qa >= 0) & (qa < quads) & (z < shards - 1))
            def _():
                pass_adjoint(qa * GROUP + i)

            return carry

        lax.fori_loop(0, GROUP, one, 0)

    def prepare(step, carry):
        ids = [step * GROUP + i for i in range(GROUP)]
        each = range(GROUP)
        qs = [q_s[h] for h in ids]
        k2 = [pair(k_s[h]) for h in ids]
        q2 = [pair(x) for x in qs]
        both = [
            fold(dot(stack(left(k), left(q)), turned(k), True)) for k, q in zip(k2, q2)
        ]
        gram = [x[:count] for x in both]
        p2 = [pair(jnp.where(lower, x[count:], 0.0)) for x in both]
        low = [jnp.where(strict, bcol_s[h] * g, 0.0) for h, g in zip(ids, gram)]
        l2 = [pair(x) for x in low]
        small = [
            jnp.sum(jnp.where(near, x, 0.0).reshape(count // TILE, TILE, count), axis=0)
            for x in low
        ]
        lane = lax.broadcasted_iota(jnp.int32, (8, count), 1)
        base = lane - lax.rem(lane, TILE)
        row8 = lax.broadcasted_iota(jnp.int32, (8, count), 0)
        parts8 = TILE // 8
        x8 = [
            [jnp.where(lane - base == row8 + 8 * p, 1.0, 0.0) for p in range(parts8)]
            for _ in each
        ]
        for j in range(TILE - 1):
            for x, m in zip(x8, small):
                pivot = x[j // 8][j % 8:j % 8 + 1]
                for p in range(j // 8, parts8):
                    column = jnp.take_along_axis(
                        m[8 * p:8 * p + 8], base + j, axis=1, mode="promise_in_bounds"
                    )
                    x[p] = x[p] - column * pivot
        x8 = [stack(*x) for x in x8]
        inv = [jnp.where(near, stack(*[x] * (count // TILE)), 0.0) for x in x8]
        for level in range(len(sizes)):
            mask = masks[level]
            i2 = [pair(x) for x in inv]
            part = [
                fold(dot(left(m), rows_of((a[0] * mask, a[1] * mask))))
                for m, a in zip(i2, l2)
            ]
            inv = [
                m - fold(dot(left(pair(x)), rows_of(n))) for m, x, n in zip(inv, part, i2)
            ]
        t2 = [pair(x) for x in inv]
        scaled = [
            left(pair(m * (1.0 / (1.0 + jnp.exp(-beta_ref[pl.ds(h, 1), :])))))
            for h, m in zip(ids, inv)
        ]
        w2 = [pair(fold(dot(t, rows_of(k)))) for t, k in zip(scaled, k2)]
        u2 = [pair(fold(dot(t, rows_of(pair(v_s[h]))))) for h, t in zip(ids, scaled)]
        onto = [stack(left(flipped(k)), left(p)) for k, p in zip(k2, p2)]
        on_w = [fold(dot(a, rows_of(w))) for a, w in zip(onto, w2)]
        on_u = [fold(dot(a, rows_of(u))) for a, u in zip(onto, u2)]
        r2 = [pair(q - x[count:]) for q, x in zip(qs, on_w)]
        n2 = [pair(x[:width]) for x in on_w]
        cots = [cot_ref[:, lanes_of(h)] for h in ids]
        back = [
            dot(stack(left(flipped(r)), left(flipped(p))), stack(c, c))
            for r, p, c in zip(r2, p2, cots)
        ]

        @pl.when(first)
        def _():
            for i, h in enumerate(ids):
                out_state[h] = encode(on_u[i][:width])
                state_copy(h).start()

        @pl.when(last)
        def _():
            for i, h in enumerate(ids):
                out_adj[h] = encode(back[i][:width])
                adj_copy(h).start()

        for i, h in enumerate(ids):
            loc_state[h] = on_u[i][:width]
            loc_adj[h] = back[i][:width]
            pu_s[h] = on_u[i][width:]
            pg_s[h] = back[i][width:]
            kp_s[h] = left(k2[i])
            qp_s[h] = left(q2[i])
            tp_s[h] = left(flipped(t2[i]))
            wp_s[h] = left(w2[i])
            up_s[h] = left(u2[i])
            rp_s[h] = left(r2[i])
            np_s[h] = left(n2[i])
            ntp_s[h] = left(flipped(n2[i]))

        @pl.when(z == 1)
        def _():
            forward(step, -1, 1)

        return carry

    lax.fori_loop(0, heads // GROUP, prepare, 0)

    def conv_back(s, h, grad):
        lanes, slot = lanes_of(h), h * 3 + s
        if s < 2:
            unit = acts[s][h]
            grad = grad - unit * jnp.sum(grad * unit, axis=1, keepdims=True)
        shift_s[slot, 8:8 + count] = grad * g_s[s, h]
        yield
        taps = [conv_ref[s, j:j + 1, lanes] for j in range(4)]
        sums = [None] * 4
        for at in range(0, count + 8, 8):
            if at == 0:
                series = before[s, :, lanes]
            elif at % 16 == 8:
                both = raws[s][at - 8:at + 8, lanes].astype(F32)
                series = both[:8]
            else:
                series = both[8:]
            full = None
            for j in range(4):
                moved = shift_s[slot, at + 3 - j:at + 11 - j]
                term, product = taps[j] * moved, series * moved
                full = term if full is None else full + term
                sums[j] = product if sums[j] is None else sums[j] + product
            if at == 0:
                edge_out[h, s * 8:s * 8 + 8, :] = full
            elif at % 16 == 8:
                held = full
            else:
                grads[s][at - 16:at, lanes] = stack(held, full).astype(BF16)
        tail[h, s * 8:s * 8 + 8, :] = full
        for j in range(4):
            cg[pl.ds((s * 4 + j) * heads + h, 1), :] = jnp.sum(sums[j], axis=0, keepdims=True)

    def state_part(h, keep):
        lanes = lanes_of(h)
        cot = cot_ref[:, lanes]
        state2 = pair(decode(in_state[h]))
        k2, q2, u2 = (halves(x, h) for x in (kp_s, qp_s, up_s))
        reads = fold(dot(stack(wp_s[h], rp_s[h]), rows_of(state2)))
        d_query = fold(dot(cot, stack(*state2), True))
        yield
        mixed_ref[:, lanes] = reads[count:] + pu_s[h]
        corr2 = pair((u2[0].astype(F32) - reads[:count]) + u2[1].astype(F32))
        yield
        ds2 = pair(jnp.where(lower, fold(dot(cot, stack(*corr2), True)), 0.0))
        yield
        d_query = d_query + fold(dot(left(ds2), rows_of(k2)))
        d_key = fold(dot(left(flipped(ds2)), rows_of(q2)))
        keep.update(state2=state2, corr2=corr2, d_key=d_key)
        yield
        yield from conv_back(0, h, d_query)

    def adjoint_part(h, keep):
        adj2 = pair(decode(in_adj[h]))
        dc2 = pair(pg_s[h] + fold(dot(kp_s[h], rows_of(adj2))))
        yield
        y_v = fold(dot(tp_s[h], rows_of(dc2)))
        keep.update(adj2=adj2, yv2=pair(y_v))
        yield
        yield from conv_back(2, h, bcol_s[h] * y_v)

    def last_part(h, keep):
        corr2, yv2 = keep["corr2"], keep["yv2"]
        ys = left(yv2)
        d_gram = jnp.where(strict, -bcol_s[h] * fold(dot(ys, turned(corr2), True)), 0.0)
        y_k = -fold(dot(ys, turned(keep["state2"]), True))
        yield
        d_key = (
            keep["d_key"] + bcol_s[h] * y_k
            + fold(dot(left(corr2), turned(keep["adj2"]), True))
            + fold(dot(left(pair(d_gram + d_gram.T)), rows_of(halves(kp_s, h))))
        )
        yield
        inner = sum(x.astype(F32) for x in yv2) * sum(x.astype(F32) for x in corr2)
        column = jnp.sum(inner, axis=1, keepdims=True)
        row = jnp.sum(jnp.where(eye, column, 0.0), axis=0, keepdims=True)
        dbeta_ref[pl.ds(h, 1), :] = row / (1.0 + jnp.exp(beta_ref[pl.ds(h, 1), :]))
        yield from conv_back(1, h, d_key)

    def together(gens):
        for _ in itertools.zip_longest(*gens):
            pass

    def chained(*gens):
        for gen in gens:
            yield from gen

    early = z < shards // 2

    def group_of(q):
        return [q * GROUP + i for i in range(GROUP)]

    def send_edges(ids):
        @pl.when(z > 0)
        def _():
            for h in ids:
                edge_copy(h).start()

    def chain(step, carry):
        ids = group_of(step)
        keeps = [{} for _ in ids]

        @pl.when(early)
        def _():
            forward(step, jnp.where(first, -1, step - 1), 2)
            together([state_part(h, keep) for h, keep in zip(ids, keeps)])
            for h, keep in zip(ids, keeps):
                sp_s[h] = left(keep["state2"])
                cp_s[h] = left(keep["corr2"])
                dk_s[h] = keep["d_key"]

        @pl.when(jnp.logical_not(early))
        def _():
            forward(-1, step, 2)
            forward(jnp.where(last, -1, step), -1, 2)
            together([adjoint_part(h, keep) for h, keep in zip(ids, keeps)])
            for h, keep in zip(ids, keeps):
                sp_s[h] = left(keep["adj2"])
                yp_s[h] = left(keep["yv2"])

        if scatter:
            @pl.when(step == 1)
            def _():
                for other in range(1, parts):
                    pl.semaphore_signal(
                        beside, inc=1, device_id=beside_of(other), device_id_type=MESH
                    )

        return carry

    lax.fori_loop(0, quads, chain, 0)

    @pl.when(early & (z > 0))
    def _():
        forward(-1, quads - 1, 2)

    def complete(step, carry):
        ids = [step * PAIR + i for i in range(PAIR)]

        @pl.when(first & (z < shards - 1))
        def _():
            for h in ids:
                adj_copy(h).wait_recv()

        @pl.when(last & (z > 1))
        def _():
            for h in ids:
                state_copy(h).wait_recv()

        @pl.when(early)
        def _():
            keeps = [
                {"state2": halves(sp_s, h), "corr2": halves(cp_s, h), "d_key": dk_s[h]}
                for h in ids
            ]
            together([
                chained(adjoint_part(h, keep), last_part(h, keep))
                for h, keep in zip(ids, keeps)
            ])

        @pl.when(jnp.logical_not(early))
        def _():
            keeps = [{"adj2": halves(sp_s, h), "yv2": halves(yp_s, h)} for h in ids]
            together([
                chained(state_part(h, keep), last_part(h, keep))
                for h, keep in zip(ids, keeps)
            ])

        send_edges(ids)
        return carry

    lax.fori_loop(0, heads // PAIR, complete, 0)

    if scatter:
        if parts > 1:
            pl.semaphore_wait(beside, parts - 1)
        piece = cgt.shape[0] // total
        cgt[...] = cg[...].T

        def cg_copy(step):
            peer, where = peer_of(step)
            return pltpu.make_async_remote_copy(
                src_ref=cgt.at[pl.ds(pl.multiple_of(peer * piece, 8), piece), :],
                dst_ref=gathered.at[step],
                send_sem=cg_send, recv_sem=cg_recv,
                device_id=where, device_id_type=MESH,
            )

        for i in range(total - 1):
            peer = jnp.where(i < mine, i, i + 1)
            cg_copy(lax.rem(peer - mine + total, total)).start()

    @pl.when(z < shards - 1)
    def _():
        all_of(edge_out, edge_in, edge_send, edge_recv, z + 1).wait_recv()

    for h in range(heads):
        for s in range(3):
            lanes = slice(h * width, (h + 1) * width)
            extra = tail[h, s * 8:s * 8 + 8, :] + edge_in[h, s * 8:s * 8 + 8, :]
            grads[s][count - 8:, lanes] = extra.astype(BF16)

    @pl.when(z < shards - 1)
    def _():
        halo_copy().wait_send()

        all_of(out_state, in_state, state_send, state_recv.at[0], z + 1).wait_send()

    @pl.when(z > 0)
    def _():
        all_of(out_adj, in_adj, adj_send, adj_recv.at[0], z - 1).wait_send()
        all_of(edge_out, edge_in, edge_send, edge_recv, z - 1).wait_send()

    if scatter:
        sums = cgt[pl.ds(pl.multiple_of(mine * piece, 8), piece), :]
        others = gathered.at[pl.ds(1, total - 1)]
        everyone = all_of(others, others, cg_send, cg_recv, lax.rem(z + 1, shards))
        everyone.wait_recv()
        for step in range(1, total):
            sums = sums + gathered[step]
        conv_out[...] = sums
        everyone.wait_send()
    else:
        conv_out[...] = cg[...]


def flush(count, *refs):
    blocks, rest = refs[:count], refs[count:]
    if len(rest) == count + 1:
        outs, sems = rest[:count], rest[count]
        extra = ()
    else:
        conv, outs, conv_out, sems, turned = rest[0], rest[1:count + 1], *rest[count + 1:]
        extra = ((turned, conv_out),)
    copies = [
        pltpu.make_async_copy(block, out, sems.at[i])
        for i, (block, out) in enumerate((*zip(blocks, outs), *extra))
    ]
    for copy in copies[:count]:
        copy.start()
    if extra:
        turned[...] = conv[...].T[:turned.shape[0]]
        copies[count].start()
    for copy in copies:
        copy.wait()


def per_device(query_raw, key_raw, value_raw, conv_weight, beta_logit, cotangent):
    shards, parts = lax.axis_size("seq"), lax.axis_size("dp")
    heads = beta_logit.shape[1]
    count, channels = query_raw.shape[1:]
    width = channels // heads
    taps = conv_weight.shape[1]
    total = shards * parts
    scatter = total > 1 and width % (8 * total) == 0
    piece = width // total if scatter else 8
    slots = total if scatter else 2
    square = lambda dtype=F32, cols=width: pltpu.VMEM((heads, count, cols), dtype)
    dma = pltpu.SemaphoreType.DMA
    vmem = pl.BlockSpec(memory_space=pltpu.VMEM)
    conv_rows = piece if scatter else width
    levels = max(1, (count // TILE - 1).bit_length())
    outs = pl.pallas_call(
        functools.partial(kernel, shards, parts, scatter),
        out_shape=(
            jax.ShapeDtypeStruct((count, channels), F32),
            jax.ShapeDtypeStruct((count, channels), BF16),
            jax.ShapeDtypeStruct((count, channels), BF16),
            jax.ShapeDtypeStruct((count, channels), BF16),
            jax.ShapeDtypeStruct((heads, count), F32),
            jax.ShapeDtypeStruct((conv_rows, 128), F32),
        ),
        in_specs=[pl.BlockSpec(memory_space=pltpu.HBM)] * 6,
        out_specs=[vmem] * 6,
        scratch_shapes=[
            pltpu.VMEM((count, channels), BF16),
            pltpu.VMEM((count, channels), BF16),
            pltpu.VMEM((count, channels), BF16),
            pltpu.VMEM((3, taps, channels), F32),
            pltpu.VMEM((heads, count), F32),
            pltpu.VMEM((count, channels), BF16),
            pltpu.VMEM((16, channels), BF16),
            pltpu.VMEM((16, channels), BF16),
            pltpu.VMEM((3, 8, channels), F32),
            square(), square(), square(),
            pltpu.VMEM((3, heads, count, width), F32),
            *[square() for _ in range(3)],
            *[square(BF16, 2 * width) for _ in range(11)],
            square(),
            pltpu.VMEM((3 * heads, count + 16, width), F32),
            pltpu.VMEM((levels, count, count), BF16),
            square(), square(),
            square(BF16), square(BF16), square(BF16), square(BF16),
            pltpu.VMEM((heads, 24, width), F32),
            pltpu.VMEM((heads, 24, width), F32),
            pltpu.VMEM((heads, 24, width), F32),
            pltpu.VMEM((128, width), F32),
            pltpu.VMEM((width, 128), F32),
            pltpu.VMEM((slots, piece, 128), F32),
            dma, dma,
            dma, dma((heads,)), dma, dma((heads,)),
            dma, dma, dma, dma, dma((6,)),
            pltpu.SemaphoreType.REGULAR,
        ],
        compiler_params=pltpu.CompilerParams(
            collective_id=0, has_side_effects=True, vmem_limit_bytes=48 << 20
        ),
    )(
        *(
            pltpu.with_memory_space_constraint(x, pltpu.HBM)
            for x in (
                query_raw[0], key_raw[0], value_raw[0],
                conv_weight, beta_logit[0], cotangent[0],
            )
        )
    )
    used = 3 * taps * heads
    blocks, conv = outs[:5], outs[5]
    held, free = pl.BlockSpec(memory_space=pl.ANY), pl.BlockSpec(memory_space=pltpu.HBM)
    extra_shape = (jax.ShapeDtypeStruct((used, piece), F32),) if scatter else ()
    flushed = pl.pallas_call(
        functools.partial(flush, 5),
        out_shape=(*(jax.ShapeDtypeStruct(x.shape, x.dtype) for x in blocks), *extra_shape),
        in_specs=[held] * 5 + [vmem] * len(extra_shape),
        out_specs=[free] * (5 + len(extra_shape)),
        scratch_shapes=[
            dma((5 + len(extra_shape),)),
            *(pltpu.VMEM(x.shape, F32) for x in extra_shape),
        ],
        compiler_params=pltpu.CompilerParams(vmem_limit_bytes=2 << 20),
    )(*blocks, *((conv,) if scatter else ()))
    mixed, d_query, d_key, d_value, d_beta = flushed[:5]
    if scatter:
        conv_grad = flushed[5].reshape(3, taps, heads, piece)
    else:
        conv_grad = lax.psum_scatter(
            conv[:used].reshape(3, taps, heads, width),
            ("seq", "dp"), scatter_dimension=3, tiled=True,
        )
    return (mixed[None], d_query[None], d_key[None], d_value[None], d_beta[None], conv_grad)


def solution(mesh):
    rows = P(("group", "dp"), "seq", "head")
    in_specs = (
        rows, rows, rows,
        P(None, None, "head"),
        P(("group", "dp"), "head", "seq"),
        rows,
    )
    out_specs = (
        rows, rows, rows, rows,
        P(("group", "dp"), "head", "seq"),
        P("group", None, "head", ("seq", "dp")),
    )
    return jax.shard_map(
        per_device, mesh=mesh, in_specs=in_specs, out_specs=out_specs, check_vma=False
    )
```
